32 devices in a mesh: layer: 8 (over y, x, core), spec: 4 (over z).
Axes of the slice: x: 2, y: 2, z: 4, core: 2. Of those that a mesh axis runs over, the one named last changes fastest.
Arguments:
- start_lead: float32 [64], P('spec'), may hold values from 128 to 512
- start_field: float32 [64, 8, 16, 1024], P('spec', 'layer'), may hold values from -6 to 6
- diag_dual: float32 [64, 8, 16, 1024], P('spec', 'layer'), may hold values from 0.25 to 2
- coupling_dual: float32 [64, 8, 16, 1024], P('spec', 'layer'), may hold values from -5 to 5
- linear_table: float32 [10, 8, 16, 1024], P(None, 'layer'), may hold values from -0.03125 to 0.03125
- labels: int32 [64], P('spec'), may hold values from 0 to 9
- bias_dual: float32 [64], P('spec'), may hold values from -1 to 1
- kernels: float32 [8, 3, 3, 64, 64], P('layer'), may hold values from -0.25 to 0.25
Outputs:
- grad_diag: float32 [64, 8, 16, 1024], P('spec', 'layer')
- grad_coupling: float32 [64, 8, 16, 1024], P('spec', 'layer')
- grad_linear: float32 [64, 8, 16, 1024], P('spec', 'layer')
- grad_bias: float32 [64], P('spec')
- soft_max: float32 [64], P('spec')
The draws below stay inside these ranges and needn't reach their ends.
All inputs are finite; a program needn't handle non-finite values.
Results may differ from the reference program's by a relative error of at most 0.0003.
Values sent between devices are 32-bit elements; how exact they have to be, the bound alone decides.
A program may use at most 128 MiB of HBM per device.

```python
import math
import jax
import jax.numpy as jnp
from jax import lax

CH = 64
SIDE = 16
CLASSES = 10
ITERS = 4
SPEC_DEV = 16
LAYERS = 8
SPECS = 64
N_SPEC = 4


def touch_ends(entries, key, smallest, largest):
    spot = [jax.random.randint(jax.random.fold_in(key, axis), (), 0, length) for axis, length in enumerate(entries.shape)]
    main_axis = entries.shape.index(max(entries.shape))
    beside = spot[:main_axis] + [(spot[main_axis] + 1) % entries.shape[main_axis]] + spot[main_axis + 1:]
    return entries.at[tuple(spot)].set(smallest).at[tuple(beside)].set(largest)


def block_levels(own_key, extent, pieces, low, largest):
    loudness = 1.0
    for dim, blocks in pieces:
        heights = jax.random.uniform(jax.random.fold_in(jax.random.fold_in(own_key, 6), dim), (blocks,), jnp.float32, low / len(pieces), largest / len(pieces))
        loudness = loudness * jnp.repeat(jnp.exp(heights), extent[dim] // blocks).reshape((-1,) + (1,) * (len(extent) - 1 - dim))
    return loudness


def scatter_about(own_key, extent, width, most, pieces=(), held_as=jnp.bfloat16):
    array = jax.random.normal(own_key, extent, jnp.float32) * width
    if len(pieces) > 0:
        array = block_levels(own_key, extent, pieces, -0.22, 0.18) * array
    return jnp.clip(array, min=-most, max=most).astype(held_as)


def setup_inputs(seed: int = 0) -> dict:
    key_list = jax.random.split(jax.random.key(seed), 9)
    start_lead = jnp.clip(128.0 + 384.0 * jax.random.uniform(key_list[0], (SPECS,), jnp.float32) ** block_levels(key_list[0], (SPECS,), ((0, 4),), -0.2, 0.2), 128.0, 512.0)
    start_field = scatter_about(key_list[1], (SPECS, LAYERS, SIDE, SIDE * CH), 1.0, 6.0, ((0, 4), (1, 8)), jnp.float32)
    diag_dual = jnp.clip(0.25 + 1.75 * jax.random.uniform(key_list[2], (SPECS, LAYERS, SIDE, SIDE * CH), jnp.float32) ** block_levels(key_list[2], (SPECS, LAYERS, SIDE, SIDE * CH), ((0, 4), (1, 8)), -0.2, 0.2), 0.25, 2.0)
    coupling_dual = scatter_about(key_list[3], (SPECS, LAYERS, SIDE, SIDE * CH), 1.0, 5.0, ((0, 4), (1, 8)), jnp.float32)
    linear_table = scatter_about(key_list[4], (CLASSES, LAYERS, SIDE, SIDE * CH), (LAYERS * SIDE * SIDE * CH // 4) ** -0.5, 0.03125, ((1, 8),), jnp.float32)
    labels = touch_ends(jax.random.randint(key_list[5], (SPECS,), 0, CLASSES), jax.random.fold_in(key_list[5], 1), 0, CLASSES - 1).astype(jnp.int32)
    bias_dual = jnp.clip(jax.random.uniform(key_list[6], (SPECS,), jnp.float32, -1.0, 1.0) * block_levels(key_list[6], (SPECS,), ((0, 4),), -0.4, 0.0), -1.0, 1.0)
    kernels = scatter_about(key_list[7], (LAYERS, 3, 3, CH, CH), (9 * CH) ** -0.5, 0.25, ((0, 8),), jnp.float32)
    return {"start_lead": start_lead, "start_field": start_field, "diag_dual": diag_dual, "coupling_dual": coupling_dual, "linear_table": linear_table, "labels": labels, "bias_dual": bias_dual, "kernels": kernels}


highest = lax.Precision.HIGHEST

def pair_blocks(kernel):
    zero_tap = jnp.zeros_like(kernel[:, 0, 0])
    per_tap = []
    for tap_row in range(3):
        side_parts = []
        for tap_side in range(3):
            row_parts = []
            for in_pos in range(2):
                col_parts = []
                for out_pos in range(2):
                    tap_col = 2 * (tap_side - 1) + in_pos - out_pos + 1
                    col_parts.append(kernel[:, tap_row, tap_col] if 0 <= tap_col <= 2 else zero_tap)
                row_parts.append(jnp.concatenate(col_parts, axis=2))
            side_parts.append(jnp.concatenate(row_parts, axis=1))
        per_tap.append(jnp.concatenate(side_parts, axis=1))
    return jnp.stack(per_tap, axis=1)

def transposed(kernel):
    return jnp.swapaxes(kernel[:, ::-1, ::-1], 3, 4)

def summed(values):
    return lax.optimization_barrier(jnp.sum(values, axis=(1, 2, 3)))

def spread(values):
    return values[:, None, None, None]

def conv_pairs(values, blocks):
    num_batch, num_layers, num_rows, num_width = values.shape
    pair_width = blocks.shape[-1]
    num_groups = num_width // pair_width
    grouped = values.reshape(num_batch, num_layers, num_rows, num_groups, pair_width)
    padded = jnp.pad(grouped, ((0, 0), (0, 0), (1, 1), (1, 1), (0, 0)))
    stacked = jnp.concatenate([padded[:, :, :, 0:num_groups], padded[:, :, :, 1:num_groups + 1], padded[:, :, :, 2:num_groups + 2]], axis=4)
    result = jnp.zeros(grouped.shape, jnp.float32)
    for tap_row in range(3):
        result = result + jnp.einsum('blhgi,lio->blhgo', stacked[:, :, tap_row:tap_row + num_rows], blocks[:, tap_row], precision=highest)
    return result.reshape(values.shape)

def local_neighbours(images, scaled):
    empty = jnp.zeros_like(images[:, :1])
    prior_img = jnp.concatenate([empty, images[:, :-1]], axis=1)
    later_in = jnp.concatenate([scaled[:, 1:], empty], axis=1)
    return (prior_img, later_in)

def apply_dual(lead_now, field_now, diag_part, coupling, linear, blocks_fwd, blocks_back, neighbours):
    images = conv_pairs(field_now, blocks_fwd)
    scaled = coupling * field_now
    prior_img, later_in = neighbours(images, scaled)
    back_img = conv_pairs(later_in, blocks_back)
    image_field = diag_part * field_now - 0.5 * coupling * prior_img - 0.5 * back_img + 0.5 * linear * spread(lead_now)
    return (image_field, prior_img)

def finish(alphas, betas, basis_lead, basis_field, basis_image, unit_count):
    alpha_mat = jnp.stack(alphas, axis=1)
    beta_mat = jnp.concatenate([jnp.stack(betas, axis=1), jnp.zeros_like(alpha_mat[:, :1])], axis=1)
    count = alpha_mat.shape[1]
    identity = jnp.eye(count, dtype=jnp.float32)
    tri_mat = alpha_mat[:, :, None] * identity + beta_mat[:, :, None] * jnp.eye(count, k=1, dtype=jnp.float32) + beta_mat[:, None, :] * jnp.eye(count, k=-1, dtype=jnp.float32)
    sigma_all = jnp.sqrt(lax.optimization_barrier(jnp.sum(tri_mat * tri_mat, axis=(1, 2))))
    scaled_tri = tri_mat / (2.0 * sigma_all[:, None, None])
    expo_mat = jnp.broadcast_to(identity, tri_mat.shape)
    for degree in range(12, 0, -1):
        expo_mat = identity + jnp.einsum('bij,bjk->bik', scaled_tri, expo_mat, precision=highest) / degree
    for squaring in range(4):
        expo_mat = jnp.einsum('bij,bjk->bik', expo_mat, expo_mat, precision=highest)
    trace_val = jnp.trace(expo_mat, axis1=1, axis2=2)
    weights = expo_mat / trace_val[:, None, None]
    soft_max = lax.optimization_barrier(jnp.sum(weights * tri_mat, axis=(1, 2)))
    lead_stack = jnp.stack(basis_lead, axis=0)
    field_stack = jnp.stack(basis_field, axis=0)
    image_stack = jnp.stack(basis_image, axis=0)
    mixed_field = jnp.einsum('bij,jblhw->iblhw', weights, field_stack, precision=highest)
    mixed_image = jnp.einsum('bij,jblhw->iblhw', weights, image_stack, precision=highest)
    grad_diag = unit_count * lax.optimization_barrier(jnp.sum(field_stack * mixed_field, axis=0))
    grad_coupling = -unit_count * lax.optimization_barrier(jnp.sum(field_stack * mixed_image, axis=0))
    grad_linear = math.sqrt(unit_count) * lax.optimization_barrier(jnp.sum(lead_stack[:, :, None, None, None] * mixed_field, axis=0))
    lead_rows = lead_stack.T
    grad_bias = lax.optimization_barrier(jnp.sum(weights * lead_rows[:, :, None] * lead_rows[:, None, :], axis=(1, 2)))
    return (grad_diag, grad_coupling, grad_linear, grad_bias, soft_max)

def lanczos(start_lead, start_field, diag_part, coupling, linear, bias_part, blocks_fwd, blocks_back):
    norm_start = start_lead * start_lead + summed(start_field * start_field)
    factor = 1.0 / jnp.sqrt(norm_start)
    lead_now = start_lead * factor
    field_now = start_field * spread(factor)
    lead_old = jnp.zeros_like(lead_now)
    field_old = jnp.zeros_like(field_now)
    beta_old = jnp.zeros_like(lead_now)
    alphas, betas, basis_lead, basis_field, basis_image = ([], [], [], [], [])
    for iteration in range(ITERS):
        image_field, prior_img = apply_dual(lead_now, field_now, diag_part, coupling, linear, blocks_fwd, blocks_back, local_neighbours)
        link_value = summed(linear * field_now)
        image_lead = bias_part * lead_now + 0.5 * link_value
        alpha_now = lead_now * image_lead + summed(field_now * image_field)
        alphas.append(alpha_now)
        basis_lead.append(lead_now)
        basis_field.append(field_now)
        basis_image.append(prior_img)
        if iteration < ITERS - 1:
            rest_lead = image_lead - alpha_now * lead_now - beta_old * lead_old
            rest_field = image_field - spread(alpha_now) * field_now - spread(beta_old) * field_old
            beta_now = jnp.sqrt(rest_lead * rest_lead + summed(rest_field * rest_field) + 1e-06)
            betas.append(beta_now)
            lead_old, field_old = (lead_now, field_now)
            lead_now = rest_lead / beta_now
            field_now = rest_field / spread(beta_now)
            beta_old = beta_now
    unit_count = start_field.shape[1] * start_field.shape[2] * start_field.shape[3]
    return finish(alphas, betas, basis_lead, basis_field, basis_image, unit_count)

def reference(start_lead, start_field, diag_dual, coupling_dual, linear_table, labels, bias_dual, kernels):
    blocks_fwd = pair_blocks(kernels)
    blocks_back = pair_blocks(transposed(kernels))

    def one_group(items):
        lead_part, field_part, diag_part, coupling, label_part, bias_part = items
        onehot = (label_part[:, None] == jnp.arange(CLASSES, dtype=jnp.int32)[None, :]).astype(jnp.float32)
        linear = jnp.einsum('sc,clhw->slhw', onehot, linear_table, precision=highest)
        return lanczos(lead_part, field_part, diag_part, coupling, linear, bias_part, blocks_fwd, blocks_back)

    def grouped(values):
        return values.reshape((N_SPEC, SPEC_DEV) + values.shape[1:])
    results = lax.map(one_group, (grouped(start_lead), grouped(start_field), grouped(diag_dual), grouped(coupling_dual), grouped(labels), grouped(bias_dual)))
    grad_diag, grad_coupling, grad_linear, grad_bias, soft_max = results
    full_shape = start_field.shape
    return (grad_diag.reshape(full_shape), grad_coupling.reshape(full_shape), grad_linear.reshape(full_shape), grad_bias.reshape(-1), soft_max.reshape(-1))
```

```python
import functools
import math

import jax
import jax.numpy as jnp
from jax import lax
from jax.experimental import pallas as pl
from jax.experimental.pallas import tpu as pltpu
from jax.sharding import PartitionSpec as P

ITERS = 4
CHUNKS = 4
LANES = 128
RELAY_SECTIONS = 8
MESH = pl.DeviceIdType.MESH


def kernel_body(
    sections,
    unit_count,
    labels,
    lead0,
    bias,
    start_hbm,
    diag_hbm,
    coup_hbm,
    table_hbm,
    kern_hbm,
    grad_diag,
    grad_coup,
    grad_lin,
    small,
    z,
    img,
    rec,
    send_img,
    send_scl,
    w_buf,
    back,
    xh,
    xl,
    wf,
    wb,
    part,
    coef,
    lead_b,
    alpha_b,
    beta_b,
    fac_b,
    pk,
    gath,
    rly,
    diag,
    coup,
    table,
    kern,
    out_d,
    out_c,
    out_l,
    s_img_s,
    s_img_r,
    s_scl_s,
    s_scl_r,
    s_pk_s,
    s_pk_r,
    s_in_s,
    s_in_r,
    s_out_s,
    s_out_r,
    s_load,
    s_one,
    s_store,
):
    me = lax.axis_index("layer")
    per, rows, width = z.shape[1:]
    num_groups = width // LANES
    half = LANES // 2
    block_rows = per * rows
    last = ITERS - 1

    barrier = pltpu.get_barrier_semaphore()
    for hop in range(1, sections):
        peer = lax.rem(me + hop, sections)
        pl.semaphore_signal(barrier, inc=1, device_id={"layer": peer}, device_id_type=MESH)

    def load_kern():
        return pltpu.make_async_copy(kern_hbm, kern, s_one.at[0])

    def load_table():
        return pltpu.make_async_copy(table_hbm, table, s_one.at[1])

    def load(which, c):
        src, dst = ((start_hbm, z), (coup_hbm, coup), (diag_hbm, diag))[which]
        return pltpu.make_async_copy(src.at[c], dst.at[c], s_load.at[which, c])

    load_kern().start()
    for c in range(CHUNKS):
        load(0, c).start()
        load(1, c).start()
    load_table().start()
    for c in range(CHUNKS):
        load(2, c).start()

    @pl.when(me == sections - 1)
    def _():
        back[0] = jnp.zeros((per, rows, width), jnp.float32)

    load_kern().wait()
    chan = kern.shape[-1]
    zero_tap = jnp.zeros((chan, chan), jnp.float32)
    for tap_row in range(3):
        fwd_taps = [kern[tap_row, tap] for tap in range(3)]
        back_taps = [jnp.transpose(kern[2 - tap_row, 2 - tap]) for tap in range(3)]
        for taps, out in ((fwd_taps, wf), (back_taps, wb)):
            for in_pos in range(4):
                pieces = [taps[in_pos - q] if 0 <= in_pos - q <= 2 else zero_tap for q in range(2)]
                val = jnp.concatenate(pieces, axis=1)
                top = val.astype(jnp.bfloat16)
                at = slice(in_pos * chan, (in_pos + 1) * chan)
                out[at, tap_row * LANES : (tap_row + 1) * LANES] = top
                out[at, (3 + tap_row) * LANES : (4 + tap_row) * LANES] = (val - top.astype(jnp.float32)).astype(jnp.bfloat16)

    relayed = sections == RELAY_SECTIONS
    low, high = sections // 2 - 1, sections // 2
    img_via, scl_via = sections - 1, 0
    direct = per // 2
    near = jnp.logical_and

    def relay_in(t, images):
        src = send_img if images else send_scl
        return pltpu.make_async_remote_copy(
            src_ref=src.at[t, pl.ds(direct, per - direct)],
            dst_ref=rly.at[t],
            send_sem=s_in_s.at[t],
            recv_sem=s_in_r.at[t],
            device_id={"layer": jnp.int32(img_via if images else scl_via)},
            device_id_type=MESH,
        )

    def relay_out(t, images):
        dst = img if images else rec
        return pltpu.make_async_remote_copy(
            src_ref=rly.at[t],
            dst_ref=dst.at[t, pl.ds(direct, per - direct)],
            send_sem=s_out_s.at[t],
            recv_sem=s_out_r.at[t],
            device_id={"layer": jnp.int32(high if images else low)},
            device_id_type=MESH,
        )

    def pass_on(t, scaled_too):
        if not relayed:
            return
        for images, via in ((False, scl_via), (True, img_via)):
            if images or scaled_too:

                @pl.when(me == via)
                def _():
                    relay_in(t, images).wait_recv()
                    relay_out(t, images).start()

    def img_copy(t, count=per):
        return pltpu.make_async_remote_copy(
            src_ref=send_img.at[t, pl.ds(0, count)],
            dst_ref=img.at[t, pl.ds(0, count)],
            send_sem=s_img_s.at[t],
            recv_sem=s_img_r.at[t],
            device_id={"layer": lax.rem(me + 1, sections)},
            device_id_type=MESH,
        )

    def scl_copy(t, count=per):
        return pltpu.make_async_remote_copy(
            src_ref=send_scl.at[t, pl.ds(0, count)],
            dst_ref=rec.at[t, pl.ds(0, count)],
            send_sem=s_scl_s.at[t],
            recv_sem=s_scl_r.at[t],
            device_id={"layer": lax.rem(me + sections - 1, sections)},
            device_id_type=MESH,
        )

    def each_copy(t, images, side, act):
        copy = img_copy if images else scl_copy
        if images:
            has = me < sections - 1 if side == 0 else me > 0
            middle = low if side == 0 else high
        else:
            has = me > 0 if side == 0 else me < sections - 1
            middle = high if side == 0 else low
        if not relayed:

            @pl.when(has)
            def _():
                act(copy(t))

            return

        @pl.when(near(has, me != middle))
        def _():
            act(copy(t))

        @pl.when(me == middle)
        def _():
            act(relay_in(t, images) if side == 0 else relay_out(t, images))
            act(copy(t, direct))

    def pk_copy(j, c, hop):
        slot = (j % 2) * CHUNKS + c
        return pltpu.make_async_remote_copy(
            src_ref=pk.at[slot],
            dst_ref=gath.at[slot, me],
            send_sem=s_pk_s.at[slot, hop],
            recv_sem=s_pk_r.at[slot, hop],
            device_id={"layer": lax.rem(me + hop, sections)},
            device_id_type=MESH,
        )

    def start_copy(copy):
        copy.start()

    def await_recv(copy):
        copy.wait_recv()

    def await_send(copy):
        copy.wait_send()

    row_id = lax.broadcasted_iota(jnp.int32, (per, LANES), 0)
    lane_id = lax.broadcasted_iota(jnp.int32, (per, LANES), 1)

    def spread_row(values, c):
        out = jnp.zeros((per, LANES), jnp.float32)
        for s in range(per):
            out = jnp.where(row_id == s, values[c * per + s], out)
        return out

    def put_shifted(s, val):
        wide = jnp.concatenate([val, jnp.zeros((rows, LANES), jnp.float32)], axis=1)
        wide = pltpu.roll(wide, half, 1)
        top = wide.astype(jnp.bfloat16)
        at = pl.ds(pl.multiple_of(s * rows, rows), rows)
        xh[at, :] = top
        xl[at, :] = (wide - top.astype(jnp.float32)).astype(jnp.bfloat16)

    def conv(wts, out_ref, t):
        row = lax.rem(lax.broadcasted_iota(jnp.int32, (block_rows, LANES), 0), rows)
        cols = [slice(g * LANES, (g + 2) * LANES) for g in range(num_groups)]
        a_hi = jnp.concatenate([xh[:, at] for at in cols], axis=0)
        a_lo = jnp.concatenate([xl[:, at] for at in cols], axis=0)
        both = jnp.dot(a_hi, wts[...], preferred_element_type=jnp.float32)
        prod = both[:, : 3 * LANES] + both[:, 3 * LANES :]
        prod += jnp.dot(a_lo, wts[:, : 3 * LANES], preferred_element_type=jnp.float32)
        for g in range(num_groups):
            mine = prod[g * block_rows : (g + 1) * block_rows]
            above = pltpu.roll(mine[:, :LANES], 1, 0)
            below = pltpu.roll(mine[:, 2 * LANES :], block_rows - 1, 0)
            out = mine[:, LANES : 2 * LANES]
            out += jnp.where(row == 0, 0.0, above)
            out += jnp.where(row == rows - 1, 0.0, below)
            out_ref[t, :, :, g * LANES : (g + 1) * LANES] = out.reshape(per, rows, LANES)

    def wide_row(k, s):
        cf = coef[k, pl.ds(s, 1), :]
        return jnp.concatenate([cf] * num_groups, axis=1)

    def fold(val):
        acc = val[:, :LANES]
        for g in range(1, num_groups):
            acc = acc + val[:, g * LANES : (g + 1) * LANES]
        return jnp.sum(acc, axis=0, keepdims=True)

    def forward(t):
        @pl.when(me < sections - 1)
        def _():
            conv(wf, send_img, t)

        each_copy(t, True, 0, start_copy)

    def recur(ref, val, j, t, s):
        val = val * wide_row(1, s) + ref[t - CHUNKS, s] * wide_row(2, s)
        if j > 1:
            val = val + ref[t - 2 * CHUNKS, s] * wide_row(3, s)
        return val

    def totals(j, c, count):
        slot = (j % 2) * CHUNKS + c
        for hop in range(1, sections):
            pk_copy(j, c, hop).wait()
        total = gath[slot, 0]
        for peer in range(1, sections):
            total = total + gath[slot, peer]
        total = jnp.broadcast_to(total, (per, LANES))
        outs = []
        for k in range(count):
            picked = jnp.where(lane_id == k * per + row_id, total, 0.0)
            outs.append(jnp.broadcast_to(jnp.sum(picked, axis=1, keepdims=True), (per, LANES)))
        return outs

    def rates(j, c):
        t = j * CHUNKS + c
        bias_c = spread_row(bias, c)
        sums = totals(j, c, 4 if j == 0 else 3)
        lead_now = lead_b[t]
        image_lead = bias_c * lead_now + 0.5 * sums[0]
        if j == 0:
            factor = 1.0 / jnp.sqrt(lead_now * lead_now + sums[3])
            fac_b[c] = factor
            alpha = factor * factor * (lead_now * image_lead + sums[1])
            lead_now = lead_now * factor
            image_lead = image_lead * factor
            power = factor * factor * sums[2]
            rest_lead = image_lead - alpha * lead_now
            beta = jnp.sqrt(image_lead * image_lead + power - alpha * alpha + 1e-06)
            lead_b[t] = lead_now
            inv = 1.0 / beta
            coef[1] = inv * factor
            coef[2] = -alpha * inv * factor
        else:
            beta_old = beta_b[t - CHUNKS]
            lead_old = lead_b[t - CHUNKS]
            alpha = lead_now * image_lead + sums[1]
            rest_lead = image_lead - alpha * lead_now - beta_old * lead_old
            beta = jnp.sqrt(image_lead * image_lead + sums[2] - alpha * alpha - beta_old * beta_old + 1e-06)
            inv = 1.0 / beta
            coef[1] = inv
            coef[2] = -alpha * inv
            coef[3] = -beta_old * inv * (fac_b[c] if j == 1 else 1.0)
        lead_b[t + CHUNKS] = rest_lead * inv
        alpha_b[t] = alpha
        beta_b[t] = beta

    def apply(j, c):
        t = j * CHUNKS + c
        final_step = j == last
        if j > 0:
            rates(j - 1, c)
        else:
            load(2, c).wait()
        coef[0] = lead_b[t]
        if not final_step:
            each_copy(t, False, 1, await_recv)

            @pl.when(me < sections - 1)
            def _():
                def shift_one(s, carry):
                    val = rec[t, s]
                    if j > 0:
                        val = recur(rec, val, j, t, s)
                        rec[t, s] = val
                    put_shifted(s, val)
                    return carry

                lax.fori_loop(0, per, shift_one, 0)
                conv(wb, back, 0)

        each_copy(t, True, 1, await_recv)

        @pl.when(me == 0)
        def _():
            img[t] = jnp.zeros((per, rows, width), jnp.float32)

        def one(s, carry):
            if j > 0:
                zs = recur(z, w_buf[c, s], j, t, s)
                z[t, s] = zs
                image = recur(img, img[t, s], j, t, s)
                img[t, s] = image
            else:
                zs = z[t, s]
                image = img[t, s]
            lin = table[labels[c * per + s]]
            if final_step:
                w = diag[c, s] * zs - coup[c, s] * image
            else:
                w = diag[c, s] * zs - 0.5 * (coup[c, s] * image + back[0, s])
            w = w + lin * (0.5 * wide_row(0, s))
            part[0, pl.ds(s, 1), :] = fold(lin * zs)
            part[1, pl.ds(s, 1), :] = fold(zs * w)
            if not final_step:
                w_buf[c, s] = w
                put_shifted(s, w)
                if j + 1 < last:
                    send_scl[t + CHUNKS, s] = coup[c, s] * w
                part[2, pl.ds(s, 1), :] = fold(w * w)
            if j == 0:
                part[3, pl.ds(s, 1), :] = fold(zs * zs)
            return carry

        lax.fori_loop(0, per, one, 0)
        if j + 1 < last:
            each_copy(t + CHUNKS, False, 0, start_copy)
        packet = jnp.zeros((per, LANES), jnp.float32)
        for k in range(4 if j == 0 else (2 if final_step else 3)):
            packet = jnp.where(lane_id == k * per + row_id, jnp.sum(part[k], axis=1, keepdims=True), packet)
        packet = jnp.sum(packet, axis=0, keepdims=True)
        slot = (j % 2) * CHUNKS + c
        pk[slot] = packet
        gath[slot, me] = packet
        for hop in range(1, sections):
            pk_copy(j, c, hop).start()

    def finish(c):
        t = last * CHUNKS + c
        bias_c = spread_row(bias, c)
        sums = totals(last, c, 2)
        lead_now = lead_b[t]
        alpha = lead_now * (bias_c * lead_now + 0.5 * sums[0]) + sums[1]
        alphas = [alpha_b[j * CHUNKS + c] for j in range(last)] + [alpha]
        betas = [beta_b[j * CHUNKS + c] for j in range(last)]
        n = ITERS
        zero = jnp.zeros((per, LANES), jnp.float32)
        tri = [[zero] * n for _ in range(n)]
        norm = zero
        for i in range(n):
            tri[i][i] = alphas[i]
            norm = norm + alphas[i] * alphas[i]
            if i + 1 < n:
                tri[i][i + 1] = betas[i]
                tri[i + 1][i] = betas[i]
                norm = norm + 2.0 * (betas[i] * betas[i])
        scale = 0.5 / jnp.sqrt(norm)
        sx = [[tri[i][k] * scale for k in range(n)] for i in range(n)]
        expo = [[zero + (1.0 if i == k else 0.0) for k in range(n)] for i in range(n)]
        for degree in range(12, 0, -1):
            nxt = []
            for i in range(n):
                line = []
                for k in range(n):
                    acc = None
                    for m in range(max(0, i - 1), min(n, i + 2)):
                        term = sx[i][m] * expo[m][k]
                        acc = term if acc is None else acc + term
                    acc = acc * (1.0 / degree)
                    line.append(acc + 1.0 if i == k else acc)
                nxt.append(line)
            expo = nxt
        for _ in range(4):
            nxt = [[None] * n for _ in range(n)]
            for i in range(n):
                for k in range(n):
                    acc = expo[i][0] * expo[0][k]
                    for m in range(1, n):
                        acc = acc + expo[i][m] * expo[m][k]
                    nxt[i][k] = acc
            expo = nxt
        trace = expo[0][0] + expo[1][1] + expo[2][2] + expo[3][3]
        inv = 1.0 / trace
        wt = [[expo[i][k] * inv for k in range(n)] for i in range(n)]
        soft = zero
        gbias = zero
        leads = [lead_b[i * CHUNKS + c] for i in range(n)]
        for i in range(n):
            for k in range(n):
                if abs(i - k) <= 1:
                    soft = soft + wt[i][k] * tri[i][k]
                gbias = gbias + wt[i][k] * (leads[i] * leads[k])
        mine = lane_id == c * per + row_id
        for k, val in enumerate((gbias, soft)):
            small[k : k + 1, :] += jnp.sum(jnp.where(mine, val, 0.0), axis=0, keepdims=True)
        fac = fac_b[c]

        def scaled_by(val, *which):
            for i in which:
                if i == 0:
                    val = val * fac
            return val

        for i in range(n):
            for k in range(n):
                coef[4 + i * n + k] = unit_count * scaled_by(wt[i][k], i, k)
        for k in range(n):
            val = wt[0][k] * leads[0]
            for i in range(1, n):
                val = val + wt[i][k] * leads[i]
            coef[4 + n * n + k] = math.sqrt(unit_count) * scaled_by(val, k)

        def final(s, carry):
            cf = [coef[4 + k, pl.ds(s, 1), :] for k in range(n * n + n)]
            for g in range(num_groups):
                cols = slice(g * LANES, (g + 1) * LANES)
                zs = [z[i * CHUNKS + c, s, :, cols] for i in range(n)]
                ims = [img[i * CHUNKS + c, s, :, cols] for i in range(n)]
                gd = gc = gl = None
                for k in range(n):
                    mixed = zs[0] * cf[k]
                    for i in range(1, n):
                        mixed = mixed + zs[i] * cf[i * n + k]
                    lin = zs[k] * cf[n * n + k]
                    if k == 0:
                        gd, gc, gl = zs[k] * mixed, -(ims[k] * mixed), lin
                    else:
                        gd, gc, gl = gd + zs[k] * mixed, gc - ims[k] * mixed, gl + lin
                out_d[c, s, :, cols] = gd
                out_c[c, s, :, cols] = gc
                out_l[c, s, :, cols] = gl
            return carry

        lax.fori_loop(0, per, final, 0)
        for which in range(3):
            store(which, c).start()

    def store(which, c):
        src, dst = ((out_d, grad_diag), (out_c, grad_coup), (out_l, grad_lin))[which]
        return pltpu.make_async_copy(src.at[c], dst.at[c], s_store.at[which, c])

    def begin(c, carry):
        lead_b[c] = spread_row(lead0, c)
        load(0, c).wait()
        load(1, c).wait()

        def first(s, carry):
            val = z[c, s]
            send_scl[c, s] = coup[c, s] * val
            put_shifted(s, val)
            return carry

        lax.fori_loop(0, per, first, 0)

        @pl.when(me < sections - 1)
        def _():
            conv(wf, send_img, c)

        @pl.when(c == 0)
        def _():
            pl.semaphore_wait(barrier, sections - 1)

        each_copy(c, False, 0, start_copy)
        each_copy(c, True, 0, start_copy)
        return carry

    small[...] = jnp.zeros((2, LANES), jnp.float32)
    lax.fori_loop(0, CHUNKS, begin, 0)
    load_table().wait()

    for j in range(last):

        def step(c, carry):
            if j == 0:
                pass_on(c, True)

                @pl.when(c > 0)
                def _():
                    pass_on(CHUNKS + c - 1, True)
            else:

                @pl.when(c > 0)
                def _():
                    pass_on((j + 1) * CHUNKS + c - 1, j + 1 < last)

                @pl.when(c == 0)
                def _():
                    pass_on((j + 1) * CHUNKS - 1, True)

            apply(j, c)
            forward((j + 1) * CHUNKS + c)
            return carry

        lax.fori_loop(0, CHUNKS, step, 0)

    pass_on(ITERS * CHUNKS - 1, False)
    apply(last, 0)

    apply(last, 1)

    def closing(c, carry):
        apply(last, c)
        finish(c - 2)
        return carry

    lax.fori_loop(2, CHUNKS, closing, 0)
    finish(CHUNKS - 2)
    finish(CHUNKS - 1)

    def settle(t, carry):
        each_copy(t, True, 0, await_send)
        if relayed:

            @pl.when(me == img_via)
            def _():
                relay_out(t, True).wait_send()

        return carry

    def settle_scaled(t, carry):
        each_copy(t, False, 0, await_send)
        if relayed:

            @pl.when(me == scl_via)
            def _():
                relay_out(t, False).wait_send()

        return carry

    lax.fori_loop(0, ITERS * CHUNKS, settle, 0)
    lax.fori_loop(0, last * CHUNKS, settle_scaled, 0)
    for c in range(CHUNKS):
        for which in range(3):
            store(which, c).wait()


def hand_over(in_d, in_c, in_l, small, out_d, out_c, out_l, gbias, soft, sems):
    moves = [
        pltpu.make_async_copy(src, dst, sems.at[which])
        for which, (src, dst) in enumerate(((in_d, out_d), (in_c, out_c), (in_l, out_l)))
    ]
    for move in moves:
        move.start()
    count = gbias.shape[0]
    gbias[...] = small[0, :count]
    soft[...] = small[1, :count]
    for move in moves:
        move.wait()


def in_hbm(array):
    return pltpu.with_memory_space_constraint(array, pltpu.HBM)


def body(start_lead, start_field, diag_dual, coupling_dual, linear_table, labels, bias_dual, kernels):
    sections = lax.axis_size("layer")
    specs, _, rows, width = start_field.shape
    unit_count = sections * rows * width
    per = specs // CHUNKS
    chan = kernels.shape[-1]
    block = (per, rows, width)
    shape = (CHUNKS,) + block
    full = pl.BlockSpec(memory_space=pltpu.VMEM)
    scalars = pl.BlockSpec(memory_space=pltpu.SMEM)
    anywhere = pl.BlockSpec(memory_space=pl.ANY)
    f32, bf16 = jnp.float32, jnp.bfloat16
    dma = pltpu.SemaphoreType.DMA
    slots, sent = ITERS * CHUNKS, (ITERS - 1) * CHUNKS
    small_block = (per, LANES)
    outs = pl.pallas_call(
        functools.partial(kernel_body, sections, float(unit_count)),
        out_shape=[pltpu.VMEM(shape, f32)] * 3 + [pltpu.VMEM((2, LANES), f32)],
        in_specs=[scalars] * 3 + [anywhere] * 5,
        out_specs=[anywhere] * 3 + [full],
        scratch_shapes=[
            pltpu.VMEM((slots,) + block, f32),
            pltpu.VMEM((slots,) + block, f32),
            pltpu.VMEM((sent,) + block, f32),
            pltpu.VMEM((slots,) + block, f32),
            pltpu.VMEM((sent,) + block, f32),
            pltpu.VMEM(shape, f32),
            pltpu.VMEM((1,) + block, f32),
            pltpu.VMEM((per * rows, width + LANES), bf16),
            pltpu.VMEM((per * rows, width + LANES), bf16),
            pltpu.VMEM((4 * chan, 12 * chan), bf16),
            pltpu.VMEM((4 * chan, 12 * chan), bf16),
            pltpu.VMEM((4,) + small_block, f32),
            pltpu.VMEM((24,) + small_block, f32),
            pltpu.VMEM((slots,) + small_block, f32),
            pltpu.VMEM((slots,) + small_block, f32),
            pltpu.VMEM((slots,) + small_block, f32),
            pltpu.VMEM((CHUNKS,) + small_block, f32),
            pltpu.VMEM((2 * CHUNKS, 1, LANES), f32),
            pltpu.VMEM((2 * CHUNKS, sections, 1, LANES), f32),
            pltpu.VMEM((slots, per - per // 2, rows, width), f32),
            pltpu.VMEM(shape, f32),
            pltpu.VMEM(shape, f32),
            pltpu.VMEM((linear_table.shape[0], rows, width), f32),
            pltpu.VMEM(kernels.shape[1:], f32),
            pltpu.VMEM(shape, f32),
            pltpu.VMEM(shape, f32),
            pltpu.VMEM(shape, f32),
            dma((slots,)),
            dma((slots,)),
            dma((sent,)),
            dma((sent,)),
            dma((2 * CHUNKS, sections)),
            dma((2 * CHUNKS, sections)),
            dma((slots,)),
            dma((slots,)),
            dma((slots,)),
            dma((slots,)),
            dma((3, CHUNKS)),
            dma((2,)),
            dma((3, CHUNKS)),
        ],
        compiler_params=pltpu.CompilerParams(collective_id=0, has_side_effects=True, vmem_limit_bytes=40 * 1024 * 1024),
    )(
        labels,
        start_lead,
        bias_dual,
        in_hbm(start_field.reshape(shape)),
        in_hbm(diag_dual.reshape(shape)),
        in_hbm(coupling_dual.reshape(shape)),
        in_hbm(linear_table.reshape(linear_table.shape[0], rows, width)),
        in_hbm(kernels.reshape(kernels.shape[1:])),
    )
    done = pl.pallas_call(
        hand_over,
        out_shape=[jax.ShapeDtypeStruct(shape, f32)] * 3 + [jax.ShapeDtypeStruct((specs,), f32)] * 2,
        in_specs=[anywhere] * 3 + [full],
        out_specs=[pl.BlockSpec(memory_space=pltpu.HBM)] * 3 + [full] * 2,
        scratch_shapes=[dma((3,))],
        compiler_params=pltpu.CompilerParams(vmem_limit_bytes=8 * 1024 * 1024),
    )(*outs)
    big = [out.reshape(start_field.shape) for out in done[:3]]
    return (*big, done[3], done[4])


def solution(mesh):
    placed = (
        P("spec"),
        P("spec", "layer", None, None),
        P("spec", "layer", None, None),
        P("spec", "layer", None, None),
        P(None, "layer", None, None),
        P("spec"),
        P("spec"),
        P("layer", None, None, None, None),
    )
    return jax.shard_map(
        body,
        mesh=mesh,
        in_specs=placed,
        out_specs=(
            P("spec", "layer", None, None),
            P("spec", "layer", None, None),
            P("spec", "layer", None, None),
            P("spec"),
            P("spec"),
        ),
        check_vma=False,
    )
```

```python
import functools
import math

import jax
import jax.numpy as jnp
from jax import lax
from jax.experimental import pallas as pl
from jax.experimental.pallas import tpu as pltpu
from jax.sharding import PartitionSpec as P

ITERS = 4
CHUNKS = 4
LANES = 128
RELAY_SECTIONS = 8
MESH = pl.DeviceIdType.MESH


def kernel_body(
    sections,
    unit_count,
    labels_hbm,
    lead0_hbm,
    bias_hbm,
    start_hbm,
    diag_hbm,
    coup_hbm,
    table_hbm,
    kern_hbm,
    grad_diag,
    grad_coup,
    grad_lin,
    small,
    z,
    img,
    rec,
    send_img,
    send_scl,
    w_buf,
    back,
    xh,
    xl,
    wf,
    wb,
    part,
    coef,
    lead_b,
    alpha_b,
    beta_b,
    fac_b,
    pk,
    gath,
    rly,
    diag,
    coup,
    table,
    kern,
    out_d,
    out_c,
    out_l,
    s_img_s,
    s_img_r,
    s_scl_s,
    s_scl_r,
    s_pk_s,
    s_pk_r,
    s_in_s,
    s_in_r,
    s_out_s,
    s_out_r,
    labels,
    lead0,
    bias,
    s_load,
    s_one,
    s_store,
):
    me = lax.axis_index("layer")
    per, rows, width = z.shape[1:]
    num_groups = width // LANES
    half = LANES // 2
    block_rows = per * rows
    last = ITERS - 1

    barrier = pltpu.get_barrier_semaphore()
    for hop in range(1, sections):
        peer = lax.rem(me + hop, sections)
        pl.semaphore_signal(barrier, inc=1, device_id={"layer": peer}, device_id_type=MESH)

    def load_kern():
        return pltpu.make_async_copy(kern_hbm, kern, s_one.at[0])

    def load_table():
        return pltpu.make_async_copy(table_hbm, table, s_one.at[1])

    def load(which, c):
        src, dst = ((start_hbm, z), (coup_hbm, coup), (diag_hbm, diag))[which]
        return pltpu.make_async_copy(src.at[c], dst.at[c], s_load.at[which, c])

    def load_row(which):
        src, dst = ((lead0_hbm, lead0), (labels_hbm, labels), (bias_hbm, bias))[which]
        return pltpu.make_async_copy(src, dst, s_one.at[2 + which])

    load_kern().start()
    for c in range(CHUNKS):
        load(0, c).start()
        load(1, c).start()
    for which in range(3):
        load_row(which).start()
    load_table().start()
    for c in range(CHUNKS):
        load(2, c).start()

    load_kern().wait()
    chan = kern.shape[-1]
    zero_tap = jnp.zeros((chan, chan), jnp.float32)

    def lay_out(taps, out, tap_row):
        for in_pos in range(4):
            pieces = [taps[in_pos - q] if 0 <= in_pos - q <= 2 else zero_tap for q in range(2)]
            val = jnp.concatenate(pieces, axis=1)
            top = val.astype(jnp.bfloat16)
            at = slice(in_pos * chan, (in_pos + 1) * chan)
            out[at, tap_row * LANES : (tap_row + 1) * LANES] = top
            out[at, (3 + tap_row) * LANES : (4 + tap_row) * LANES] = (val - top.astype(jnp.float32)).astype(jnp.bfloat16)

    for tap_row in range(3):
        lay_out([kern[tap_row, tap] for tap in range(3)], wf, tap_row)

    relayed = sections == RELAY_SECTIONS
    low, high = sections // 2 - 1, sections // 2
    img_via, scl_via = sections - 1, 0
    direct = per // 2
    near = jnp.logical_and

    def relay_in(t, images):
        src = send_img if images else send_scl
        return pltpu.make_async_remote_copy(
            src_ref=src.at[t, pl.ds(direct, per - direct)],
            dst_ref=rly.at[t],
            send_sem=s_in_s.at[t],
            recv_sem=s_in_r.at[t],
            device_id={"layer": jnp.int32(img_via if images else scl_via)},
            device_id_type=MESH,
        )

    def relay_out(t, images):
        dst = img if images else rec
        return pltpu.make_async_remote_copy(
            src_ref=rly.at[t],
            dst_ref=dst.at[t, pl.ds(direct, per - direct)],
            send_sem=s_out_s.at[t],
            recv_sem=s_out_r.at[t],
            device_id={"layer": jnp.int32(high if images else low)},
            device_id_type=MESH,
        )

    def pass_on(t, scaled_too):
        if not relayed:
            return
        for images, via in ((False, scl_via), (True, img_via)):
            if images or scaled_too:

                @pl.when(me == via)
                def _():
                    relay_in(t, images).wait_recv()
                    relay_out(t, images).start()

    def img_copy(t, count=per):
        return pltpu.make_async_remote_copy(
            src_ref=send_img.at[t, pl.ds(0, count)],
            dst_ref=img.at[t, pl.ds(0, count)],
            send_sem=s_img_s.at[t],
            recv_sem=s_img_r.at[t],
            device_id={"layer": lax.rem(me + 1, sections)},
            device_id_type=MESH,
        )

    def scl_copy(t, count=per):
        return pltpu.make_async_remote_copy(
            src_ref=send_scl.at[t, pl.ds(0, count)],
            dst_ref=rec.at[t, pl.ds(0, count)],
            send_sem=s_scl_s.at[t],
            recv_sem=s_scl_r.at[t],
            device_id={"layer": lax.rem(me + sections - 1, sections)},
            device_id_type=MESH,
        )

    def each_copy(t, images, side, act):
        copy = img_copy if images else scl_copy
        if images:
            has = me < sections - 1 if side == 0 else me > 0
            middle = low if side == 0 else high
        else:
            has = me > 0 if side == 0 else me < sections - 1
            middle = high if side == 0 else low
        if not relayed:

            @pl.when(has)
            def _():
                act(copy(t))

            return

        @pl.when(near(has, me != middle))
        def _():
            act(copy(t))

        @pl.when(me == middle)
        def _():
            act(relay_in(t, images) if side == 0 else relay_out(t, images))
            act(copy(t, direct))

    def pk_copy(j, c, hop):
        slot = (j % 2) * CHUNKS + c
        return pltpu.make_async_remote_copy(
            src_ref=pk.at[slot],
            dst_ref=gath.at[slot, me],
            send_sem=s_pk_s.at[slot, hop],
            recv_sem=s_pk_r.at[slot, hop],
            device_id={"layer": lax.rem(me + hop, sections)},
            device_id_type=MESH,
        )

    def start_copy(copy):
        copy.start()

    def await_recv(copy):
        copy.wait_recv()

    def await_send(copy):
        copy.wait_send()

    row_id = lax.broadcasted_iota(jnp.int32, (per, LANES), 0)
    lane_id = lax.broadcasted_iota(jnp.int32, (per, LANES), 1)

    def spread_row(values, c):
        out = jnp.zeros((per, LANES), jnp.float32)
        for s in range(per):
            out = jnp.where(row_id == s, values[c * per + s], out)
        return out

    def put_shifted(s, val):
        wide = jnp.concatenate([val, jnp.zeros((rows, LANES), jnp.float32)], axis=1)
        wide = pltpu.roll(wide, half, 1)
        top = wide.astype(jnp.bfloat16)
        at = pl.ds(pl.multiple_of(s * rows, rows), rows)
        xh[at, :] = top
        xl[at, :] = (wide - top.astype(jnp.float32)).astype(jnp.bfloat16)

    def conv(wts, out_ref, t):
        row = lax.rem(lax.broadcasted_iota(jnp.int32, (block_rows, LANES), 0), rows)
        cols = [slice(g * LANES, (g + 2) * LANES) for g in range(num_groups)]
        a_hi = jnp.concatenate([xh[:, at] for at in cols], axis=0)
        a_lo = jnp.concatenate([xl[:, at] for at in cols], axis=0)
        both = jnp.dot(a_hi, wts[...], preferred_element_type=jnp.float32)
        prod = both[:, : 3 * LANES] + both[:, 3 * LANES :]
        prod += jnp.dot(a_lo, wts[:, : 3 * LANES], preferred_element_type=jnp.float32)
        for g in range(num_groups):
            mine = prod[g * block_rows : (g + 1) * block_rows]
            above = pltpu.roll(mine[:, :LANES], 1, 0)
            below = pltpu.roll(mine[:, 2 * LANES :], block_rows - 1, 0)
            out = mine[:, LANES : 2 * LANES]
            out += jnp.where(row == 0, 0.0, above)
            out += jnp.where(row == rows - 1, 0.0, below)
            out_ref[t, :, :, g * LANES : (g + 1) * LANES] = out.reshape(per, rows, LANES)

    def wide_row(k, s):
        cf = coef[k, pl.ds(s, 1), :]
        return jnp.concatenate([cf] * num_groups, axis=1)

    def fold(val):
        acc = val[:, :LANES]
        for g in range(1, num_groups):
            acc = acc + val[:, g * LANES : (g + 1) * LANES]
        return jnp.sum(acc, axis=0, keepdims=True)

    def forward(t):
        @pl.when(me < sections - 1)
        def _():
            conv(wf, send_img, t)

        each_copy(t, True, 0, start_copy)

    def recur(ref, val, j, t, s):
        val = val * wide_row(1, s) + ref[t - CHUNKS, s] * wide_row(2, s)
        if j > 1:
            val = val + ref[t - 2 * CHUNKS, s] * wide_row(3, s)
        return val

    def totals(j, c, count):
        slot = (j % 2) * CHUNKS + c
        for hop in range(1, sections):
            pk_copy(j, c, hop).wait()
        total = gath[slot, 0]
        for peer in range(1, sections):
            total = total + gath[slot, peer]
        total = jnp.broadcast_to(total, (per, LANES))
        outs = []
        for k in range(count):
            picked = jnp.where(lane_id == k * per + row_id, total, 0.0)
            outs.append(jnp.broadcast_to(jnp.sum(picked, axis=1, keepdims=True), (per, LANES)))
        return outs

    def rates(j, c):
        t = j * CHUNKS + c
        bias_c = spread_row(bias, c)
        sums = totals(j, c, 4 if j == 0 else 3)
        lead_now = lead_b[t]
        image_lead = bias_c * lead_now + 0.5 * sums[0]
        if j == 0:
            factor = 1.0 / jnp.sqrt(lead_now * lead_now + sums[3])
            fac_b[c] = factor
            alpha = factor * factor * (lead_now * image_lead + sums[1])
            lead_now = lead_now * factor
            image_lead = image_lead * factor
            power = factor * factor * sums[2]
            rest_lead = image_lead - alpha * lead_now
            beta = jnp.sqrt(image_lead * image_lead + power - alpha * alpha + 1e-06)
            lead_b[t] = lead_now
            inv = 1.0 / beta
            coef[1] = inv * factor
            coef[2] = -alpha * inv * factor
        else:
            beta_old = beta_b[t - CHUNKS]
            lead_old = lead_b[t - CHUNKS]
            alpha = lead_now * image_lead + sums[1]
            rest_lead = image_lead - alpha * lead_now - beta_old * lead_old
            beta = jnp.sqrt(image_lead * image_lead + sums[2] - alpha * alpha - beta_old * beta_old + 1e-06)
            inv = 1.0 / beta
            coef[1] = inv
            coef[2] = -alpha * inv
            coef[3] = -beta_old * inv * (fac_b[c] if j == 1 else 1.0)
        lead_b[t + CHUNKS] = rest_lead * inv
        alpha_b[t] = alpha
        beta_b[t] = beta

    def apply(j, c):
        t = j * CHUNKS + c
        final_step = j == last
        if not final_step:
            each_copy(t, False, 1, await_recv)

            @pl.when(me < sections - 1)
            def _():
                def shift_one(s, carry):
                    put_shifted(s, rec[t, s])
                    return carry

                lax.fori_loop(0, per, shift_one, 0)
                conv(wb, back, t)

            @pl.when(me == sections - 1)
            def _():
                back[t] = jnp.zeros((per, rows, width), jnp.float32)

        if j > 0:
            rates(j - 1, c)
        else:
            load(2, c).wait()
        coef[0] = lead_b[t]
        each_copy(t, True, 1, await_recv)

        @pl.when(me == 0)
        def _():
            img[t] = jnp.zeros((per, rows, width), jnp.float32)

        def one(s, carry):
            if j > 0:
                zs = recur(z, w_buf[c, s], j, t, s)
                z[t, s] = zs
                image = recur(img, img[t, s], j, t, s)
                img[t, s] = image
            else:
                zs = z[t, s]
                image = img[t, s]
            lin = table[labels[c * per + s]]
            if final_step:
                w = diag[c, s] * zs - coup[c, s] * image
            else:
                pulled = back[t, s]
                if j > 0:
                    pulled = recur(back, pulled, j, t, s)
                    if j + 1 < last:
                        back[t, s] = pulled
                w = diag[c, s] * zs - 0.5 * (coup[c, s] * image + pulled)
            w = w + lin * (0.5 * wide_row(0, s))
            part[0, pl.ds(s, 1), :] = fold(lin * zs)
            part[1, pl.ds(s, 1), :] = fold(zs * w)
            if not final_step:
                w_buf[c, s] = w
                put_shifted(s, w)
                if j + 1 < last:
                    send_scl[t + CHUNKS, s] = coup[c, s] * w
                part[2, pl.ds(s, 1), :] = fold(w * w)
            if j == 0:
                part[3, pl.ds(s, 1), :] = fold(zs * zs)
            return carry

        lax.fori_loop(0, per, one, 0)
        if j + 1 < last:
            each_copy(t + CHUNKS, False, 0, start_copy)
        packet = jnp.zeros((per, LANES), jnp.float32)
        for k in range(4 if j == 0 else (2 if final_step else 3)):
            packet = jnp.where(lane_id == k * per + row_id, jnp.sum(part[k], axis=1, keepdims=True), packet)
        packet = jnp.sum(packet, axis=0, keepdims=True)
        slot = (j % 2) * CHUNKS + c
        pk[slot] = packet
        gath[slot, me] = packet
        for hop in range(1, sections):
            pk_copy(j, c, hop).start()

    def finish(c):
        t = last * CHUNKS + c
        bias_c = spread_row(bias, c)
        sums = totals(last, c, 2)
        lead_now = lead_b[t]
        alpha = lead_now * (bias_c * lead_now + 0.5 * sums[0]) + sums[1]
        alphas = [alpha_b[j * CHUNKS + c] for j in range(last)] + [alpha]
        betas = [beta_b[j * CHUNKS + c] for j in range(last)]
        n = ITERS
        zero = jnp.zeros((per, LANES), jnp.float32)
        tri = [[zero] * n for _ in range(n)]
        norm = zero
        for i in range(n):
            tri[i][i] = alphas[i]
            norm = norm + alphas[i] * alphas[i]
            if i + 1 < n:
                tri[i][i + 1] = betas[i]
                tri[i + 1][i] = betas[i]
                norm = norm + 2.0 * (betas[i] * betas[i])
        scale = 0.5 / jnp.sqrt(norm)
        sx = [[tri[i][k] * scale for k in range(n)] for i in range(n)]
        expo = [[zero + (1.0 if i == k else 0.0) for k in range(n)] for i in range(n)]
        for degree in range(12, 0, -1):
            nxt = []
            for i in range(n):
                line = []
                for k in range(n):
                    acc = None
                    for m in range(max(0, i - 1), min(n, i + 2)):
                        term = sx[i][m] * expo[m][k]
                        acc = term if acc is None else acc + term
                    acc = acc * (1.0 / degree)
                    line.append(acc + 1.0 if i == k else acc)
                nxt.append(line)
            expo = nxt
        for _ in range(4):
            nxt = [[None] * n for _ in range(n)]
            for i in range(n):
                for k in range(n):
                    acc = expo[i][0] * expo[0][k]
                    for m in range(1, n):
                        acc = acc + expo[i][m] * expo[m][k]
                    nxt[i][k] = acc
            expo = nxt
        trace = expo[0][0] + expo[1][1] + expo[2][2] + expo[3][3]
        inv = 1.0 / trace
        wt = [[expo[i][k] * inv for k in range(n)] for i in range(n)]
        soft = zero
        gbias = zero
        leads = [lead_b[i * CHUNKS + c] for i in range(n)]
        for i in range(n):
            for k in range(n):
                if abs(i - k) <= 1:
                    soft = soft + wt[i][k] * tri[i][k]
                gbias = gbias + wt[i][k] * (leads[i] * leads[k])
        mine = lane_id == c * per + row_id
        for k, val in enumerate((gbias, soft)):
            small[k : k + 1, :] += jnp.sum(jnp.where(mine, val, 0.0), axis=0, keepdims=True)
        fac = fac_b[c]

        def scaled_by(val, *which):
            for i in which:
                if i == 0:
                    val = val * fac
            return val

        for i in range(n):
            for k in range(n):
                coef[4 + i * n + k] = unit_count * scaled_by(wt[i][k], i, k)
        for k in range(n):
            val = wt[0][k] * leads[0]
            for i in range(1, n):
                val = val + wt[i][k] * leads[i]
            coef[4 + n * n + k] = math.sqrt(unit_count) * scaled_by(val, k)

        def final(s, carry):
            cf = [coef[4 + k, pl.ds(s, 1), :] for k in range(n * n + n)]
            for g in range(num_groups):
                cols = slice(g * LANES, (g + 1) * LANES)
                zs = [z[i * CHUNKS + c, s, :, cols] for i in range(n)]
                ims = [img[i * CHUNKS + c, s, :, cols] for i in range(n)]
                gd = gc = gl = None
                for k in range(n):
                    mixed = zs[0] * cf[k]
                    for i in range(1, n):
                        mixed = mixed + zs[i] * cf[i * n + k]
                    lin = zs[k] * cf[n * n + k]
                    if k == 0:
                        gd, gc, gl = zs[k] * mixed, -(ims[k] * mixed), lin
                    else:
                        gd, gc, gl = gd + zs[k] * mixed, gc - ims[k] * mixed, gl + lin
                out_d[c, s, :, cols] = gd
                out_c[c, s, :, cols] = gc
                out_l[c, s, :, cols] = gl
            return carry

        lax.fori_loop(0, per, final, 0)
        for which in range(3):
            store(which, c).start()

    def store(which, c):
        src, dst = ((out_d, grad_diag), (out_c, grad_coup), (out_l, grad_lin))[which]
        return pltpu.make_async_copy(src.at[c], dst.at[c], s_store.at[which, c])

    def begin(c, carry):
        load(0, c).wait()
        load(1, c).wait()

        def first(s, carry):
            val = z[c, s]
            send_scl[c, s] = coup[c, s] * val
            put_shifted(s, val)
            return carry

        lax.fori_loop(0, per, first, 0)

        @pl.when(me < sections - 1)
        def _():
            conv(wf, send_img, c)

        @pl.when(c == 0)
        def _():
            pl.semaphore_wait(barrier, sections - 1)

        each_copy(c, False, 0, start_copy)
        each_copy(c, True, 0, start_copy)
        return carry

    small[...] = jnp.zeros((2, LANES), jnp.float32)
    lax.fori_loop(0, CHUNKS, begin, 0)
    for tap_row in range(3):
        lay_out([jnp.transpose(kern[2 - tap_row, 2 - tap]) for tap in range(3)], wb, tap_row)
    load_table().wait()
    for which in range(3):
        load_row(which).wait()

    def spread_lead(c, carry):
        lead_b[c] = spread_row(lead0, c)
        return carry

    lax.fori_loop(0, CHUNKS, spread_lead, 0)

    def pass_first(c, carry):
        pass_on(c, True)
        return carry

    lax.fori_loop(0, CHUNKS, pass_first, 0)

    for j in range(last):

        def step(c, carry):
            @pl.when(c > 0)
            def _():
                pass_on((j + 1) * CHUNKS + c - 1, j + 1 < last)

            if j > 0:

                @pl.when(c == 0)
                def _():
                    pass_on((j + 1) * CHUNKS - 1, True)

            apply(j, c)
            forward((j + 1) * CHUNKS + c)
            return carry

        lax.fori_loop(0, CHUNKS, step, 0)

    pass_on(ITERS * CHUNKS - 1, False)

    def closing(c, carry):
        apply(last, c)
        return carry

    def ending(c, carry):
        finish(c)
        return carry

    lax.fori_loop(0, CHUNKS, closing, 0)
    lax.fori_loop(0, CHUNKS, ending, 0)

    def settle(t, carry):
        each_copy(t, True, 0, await_send)
        if relayed:

            @pl.when(me == img_via)
            def _():
                relay_out(t, True).wait_send()

        return carry

    def settle_scaled(t, carry):
        each_copy(t, False, 0, await_send)
        if relayed:

            @pl.when(me == scl_via)
            def _():
                relay_out(t, False).wait_send()

        return carry

    lax.fori_loop(0, ITERS * CHUNKS, settle, 0)
    lax.fori_loop(0, last * CHUNKS, settle_scaled, 0)
    for c in range(CHUNKS):
        for which in range(3):
            store(which, c).wait()


def hand_over(in_d, in_c, in_l, small, out_d, out_c, out_l, gbias, soft, sums, row_b, row_s, sems):
    moves = [
        pltpu.make_async_copy(src, dst, sems.at[which])
        for which, (src, dst) in enumerate(((in_d, out_d), (in_c, out_c), (in_l, out_l)))
    ]
    fetch = pltpu.make_async_copy(small, sums, sems.at[3])
    fetch.start()
    for move in moves:
        move.start()
    fetch.wait()
    count = gbias.shape[0]
    row_b[...] = sums[0, :count]
    row_s[...] = sums[1, :count]
    rows = [pltpu.make_async_copy(row_b, gbias, sems.at[4]), pltpu.make_async_copy(row_s, soft, sems.at[5])]
    for row in rows:
        row.start()
    for move in moves + rows:
        move.wait()


def in_hbm(array):
    return pltpu.with_memory_space_constraint(array, pltpu.HBM)


def body(start_lead, start_field, diag_dual, coupling_dual, linear_table, labels, bias_dual, kernels):
    sections = lax.axis_size("layer")
    specs, _, rows, width = start_field.shape
    unit_count = sections * rows * width
    per = specs // CHUNKS
    chan = kernels.shape[-1]
    block = (per, rows, width)
    shape = (CHUNKS,) + block
    full = pl.BlockSpec(memory_space=pltpu.VMEM)
    anywhere = pl.BlockSpec(memory_space=pl.ANY)
    f32, bf16 = jnp.float32, jnp.bfloat16
    dma = pltpu.SemaphoreType.DMA
    slots, sent = ITERS * CHUNKS, (ITERS - 1) * CHUNKS
    small_block = (per, LANES)
    outs = pl.pallas_call(
        functools.partial(kernel_body, sections, float(unit_count)),
        out_shape=[pltpu.VMEM(shape, f32)] * 3 + [pltpu.VMEM((2, LANES), f32)],
        in_specs=[anywhere] * 8,
        out_specs=[anywhere] * 3 + [full],
        scratch_shapes=[
            pltpu.VMEM((slots,) + block, f32),
            pltpu.VMEM((slots,) + block, f32),
            pltpu.VMEM((sent,) + block, f32),
            pltpu.VMEM((slots,) + block, f32),
            pltpu.VMEM((sent,) + block, f32),
            pltpu.VMEM(shape, f32),
            pltpu.VMEM((sent,) + block, f32),
            pltpu.VMEM((per * rows, width + LANES), bf16),
            pltpu.VMEM((per * rows, width + LANES), bf16),
            pltpu.VMEM((4 * chan, 12 * chan), bf16),
            pltpu.VMEM((4 * chan, 12 * chan), bf16),
            pltpu.VMEM((4,) + small_block, f32),
            pltpu.VMEM((24,) + small_block, f32),
            pltpu.VMEM((slots,) + small_block, f32),
            pltpu.VMEM((slots,) + small_block, f32),
            pltpu.VMEM((slots,) + small_block, f32),
            pltpu.VMEM((CHUNKS,) + small_block, f32),
            pltpu.VMEM((2 * CHUNKS, 1, LANES), f32),
            pltpu.VMEM((2 * CHUNKS, sections, 1, LANES), f32),
            pltpu.VMEM((slots, per - per // 2, rows, width), f32),
            pltpu.VMEM(shape, f32),
            pltpu.VMEM(shape, f32),
            pltpu.VMEM((linear_table.shape[0], rows, width), f32),
            pltpu.VMEM(kernels.shape[1:], f32),
            pltpu.VMEM(shape, f32),
            pltpu.VMEM(shape, f32),
            pltpu.VMEM(shape, f32),
            dma((slots,)),
            dma((slots,)),
            dma((sent,)),
            dma((sent,)),
            dma((2 * CHUNKS, sections)),
            dma((2 * CHUNKS, sections)),
            dma((slots,)),
            dma((slots,)),
            dma((slots,)),
            dma((slots,)),
            pltpu.SMEM((specs,), jnp.int32),
            pltpu.SMEM((specs,), f32),
            pltpu.SMEM((specs,), f32),
            dma((3, CHUNKS)),
            dma((5,)),
            dma((3, CHUNKS)),
        ],
        compiler_params=pltpu.CompilerParams(collective_id=0, has_side_effects=True, vmem_limit_bytes=44 * 1024 * 1024),
    )(
        in_hbm(labels),
        in_hbm(start_lead),
        in_hbm(bias_dual),
        in_hbm(start_field.reshape(shape)),
        in_hbm(diag_dual.reshape(shape)),
        in_hbm(coupling_dual.reshape(shape)),
        in_hbm(linear_table.reshape(linear_table.shape[0], rows, width)),
        in_hbm(kernels.reshape(kernels.shape[1:])),
    )
    done = pl.pallas_call(
        hand_over,
        out_shape=[jax.ShapeDtypeStruct(shape, f32)] * 3 + [jax.ShapeDtypeStruct((specs,), f32)] * 2,
        in_specs=[anywhere] * 4,
        out_specs=[anywhere] * 5,
        scratch_shapes=[pltpu.VMEM((2, LANES), f32), pltpu.VMEM((specs,), f32), pltpu.VMEM((specs,), f32), dma((6,))],
        compiler_params=pltpu.CompilerParams(vmem_limit_bytes=8 * 1024 * 1024),
    )(*outs)
    big = [out.reshape(start_field.shape) for out in done[:3]]
    return (*big, done[3], done[4])


def solution(mesh):
    placed = (
        P("spec"),
        P("spec", "layer", None, None),
        P("spec", "layer", None, None),
        P("spec", "layer", None, None),
        P(None, "layer", None, None),
        P("spec"),
        P("spec"),
        P("layer", None, None, None, None),
    )
    return jax.shard_map(
        body,
        mesh=mesh,
        in_specs=placed,
        out_specs=(
            P("spec", "layer", None, None),
            P("spec", "layer", None, None),
            P("spec", "layer", None, None),
            P("spec"),
            P("spec"),
        ),
        check_vma=False,
    )
```

```python
import functools
import math

import jax
import jax.numpy as jnp
from jax import lax
from jax.experimental import pallas as pl
from jax.experimental.pallas import tpu as pltpu
from jax.sharding import PartitionSpec as P

ITERS = 4
CHUNKS = 4
LANES = 128
RELAY_SECTIONS = 8
MESH = pl.DeviceIdType.MESH


def kernel_body(
    sections,
    unit_count,
    labels_hbm,
    lead0_hbm,
    bias_hbm,
    start_hbm,
    diag_hbm,
    coup_hbm,
    table_hbm,
    kern_hbm,
    grad_diag,
    grad_coup,
    grad_lin,
    small,
    z,
    img,
    rec,
    send_img,
    send_scl,
    w_buf,
    back,
    xh,
    xl,
    wf,
    wb,
    part,
    coef,
    lead_b,
    alpha_b,
    beta_b,
    fac_b,
    pk,
    gath,
    rly,
    diag,
    coup,
    table,
    kern,
    s_img_s,
    s_img_r,
    s_scl_s,
    s_scl_r,
    s_pk_s,
    s_pk_r,
    s_in_s,
    s_in_r,
    s_out_s,
    s_out_r,
    labels,
    lead0,
    bias,
    s_load,
    s_one,
):
    me = lax.axis_index("layer")
    per, rows, width = z.shape[1:]
    num_groups = width // LANES
    half = LANES // 2
    block_rows = per * rows
    last = ITERS - 1

    barrier = pltpu.get_barrier_semaphore()
    for hop in range(1, sections):
        peer = lax.rem(me + hop, sections)
        pl.semaphore_signal(barrier, inc=1, device_id={"layer": peer}, device_id_type=MESH)

    def load_kern():
        return pltpu.make_async_copy(kern_hbm, kern, s_one.at[0])

    def load_table():
        return pltpu.make_async_copy(table_hbm, table, s_one.at[1])

    def load(which, c):
        src, dst = ((start_hbm, z), (coup_hbm, coup), (diag_hbm, diag))[which]
        return pltpu.make_async_copy(src.at[c], dst.at[c], s_load.at[which, c])

    def load_row(which):
        src, dst = ((lead0_hbm, lead0), (labels_hbm, labels), (bias_hbm, bias))[which]
        return pltpu.make_async_copy(src, dst, s_one.at[2 + which])

    load_kern().start()
    for c in range(CHUNKS):
        load(0, c).start()
        load(1, c).start()
    for which in range(3):
        load_row(which).start()
    load_table().start()
    for c in range(CHUNKS):
        load(2, c).start()

    load_kern().wait()
    chan = kern.shape[-1]
    zero_tap = jnp.zeros((chan, chan), jnp.float32)

    def lay_out(taps, out, tap_row):
        for in_pos in range(4):
            pieces = [taps[in_pos - q] if 0 <= in_pos - q <= 2 else zero_tap for q in range(2)]
            val = jnp.concatenate(pieces, axis=1)
            top = val.astype(jnp.bfloat16)
            at = slice(in_pos * chan, (in_pos + 1) * chan)
            out[at, tap_row * LANES : (tap_row + 1) * LANES] = top
            out[at, (3 + tap_row) * LANES : (4 + tap_row) * LANES] = (val - top.astype(jnp.float32)).astype(jnp.bfloat16)

    for tap_row in range(3):
        lay_out([kern[tap_row, tap] for tap in range(3)], wf, tap_row)

    relayed = sections == RELAY_SECTIONS
    low, high = sections // 2 - 1, sections // 2
    img_via, scl_via = sections - 1, 0
    direct = per // 2
    near = jnp.logical_and

    def relay_in(t, images):
        src = send_img if images else send_scl
        return pltpu.make_async_remote_copy(
            src_ref=src.at[t, pl.ds(direct, per - direct)],
            dst_ref=rly.at[t],
            send_sem=s_in_s.at[t],
            recv_sem=s_in_r.at[t],
            device_id={"layer": jnp.int32(img_via if images else scl_via)},
            device_id_type=MESH,
        )

    def relay_out(t, images):
        dst = img if images else rec
        return pltpu.make_async_remote_copy(
            src_ref=rly.at[t],
            dst_ref=dst.at[t, pl.ds(direct, per - direct)],
            send_sem=s_out_s.at[t],
            recv_sem=s_out_r.at[t],
            device_id={"layer": jnp.int32(high if images else low)},
            device_id_type=MESH,
        )

    def pass_on(t, scaled_too):
        if not relayed:
            return
        for images, via in ((False, scl_via), (True, img_via)):
            if images or scaled_too:

                @pl.when(me == via)
                def _():
                    relay_in(t, images).wait_recv()
                    relay_out(t, images).start()

    def img_copy(t, count=per):
        return pltpu.make_async_remote_copy(
            src_ref=send_img.at[t, pl.ds(0, count)],
            dst_ref=img.at[t, pl.ds(0, count)],
            send_sem=s_img_s.at[t],
            recv_sem=s_img_r.at[t],
            device_id={"layer": lax.rem(me + 1, sections)},
            device_id_type=MESH,
        )

    def scl_copy(t, count=per):
        return pltpu.make_async_remote_copy(
            src_ref=send_scl.at[t, pl.ds(0, count)],
            dst_ref=rec.at[t, pl.ds(0, count)],
            send_sem=s_scl_s.at[t],
            recv_sem=s_scl_r.at[t],
            device_id={"layer": lax.rem(me + sections - 1, sections)},
            device_id_type=MESH,
        )

    def each_copy(t, images, side, act):
        copy = img_copy if images else scl_copy
        if images:
            has = me < sections - 1 if side == 0 else me > 0
            middle = low if side == 0 else high
        else:
            has = me > 0 if side == 0 else me < sections - 1
            middle = high if side == 0 else low
        if not relayed:

            @pl.when(has)
            def _():
                act(copy(t))

            return

        @pl.when(near(has, me != middle))
        def _():
            act(copy(t))

        @pl.when(me == middle)
        def _():
            act(relay_in(t, images) if side == 0 else relay_out(t, images))
            act(copy(t, direct))

    def pk_copy(j, c, hop):
        slot = (j % 2) * CHUNKS + c
        return pltpu.make_async_remote_copy(
            src_ref=pk.at[slot],
            dst_ref=gath.at[slot, me],
            send_sem=s_pk_s.at[slot, hop],
            recv_sem=s_pk_r.at[slot, hop],
            device_id={"layer": lax.rem(me + hop, sections)},
            device_id_type=MESH,
        )

    def start_copy(copy):
        copy.start()

    def await_recv(copy):
        copy.wait_recv()

    def await_send(copy):
        copy.wait_send()

    row_id = lax.broadcasted_iota(jnp.int32, (per, LANES), 0)
    lane_id = lax.broadcasted_iota(jnp.int32, (per, LANES), 1)

    def spread_row(values, c):
        out = jnp.zeros((per, LANES), jnp.float32)
        for s in range(per):
            out = jnp.where(row_id == s, values[c * per + s], out)
        return out

    def put_shifted(s, val):
        wide = jnp.concatenate([val, jnp.zeros((rows, LANES), jnp.float32)], axis=1)
        wide = pltpu.roll(wide, half, 1)
        top = wide.astype(jnp.bfloat16)
        at = pl.ds(pl.multiple_of(s * rows, rows), rows)
        xh[at, :] = top
        xl[at, :] = (wide - top.astype(jnp.float32)).astype(jnp.bfloat16)

    def conv(wts, out_ref, t):
        row = lax.rem(lax.broadcasted_iota(jnp.int32, (block_rows, LANES), 0), rows)
        cols = [slice(g * LANES, (g + 2) * LANES) for g in range(num_groups)]
        a_hi = jnp.concatenate([xh[:, at] for at in cols], axis=0)
        a_lo = jnp.concatenate([xl[:, at] for at in cols], axis=0)
        both = jnp.dot(a_hi, wts[...], preferred_element_type=jnp.float32)
        prod = both[:, : 3 * LANES] + both[:, 3 * LANES :]
        prod += jnp.dot(a_lo, wts[:, : 3 * LANES], preferred_element_type=jnp.float32)
        for g in range(num_groups):
            mine = prod[g * block_rows : (g + 1) * block_rows]
            above = pltpu.roll(mine[:, :LANES], 1, 0)
            below = pltpu.roll(mine[:, 2 * LANES :], block_rows - 1, 0)
            out = mine[:, LANES : 2 * LANES]
            out += jnp.where(row == 0, 0.0, above)
            out += jnp.where(row == rows - 1, 0.0, below)
            out_ref[t, :, :, g * LANES : (g + 1) * LANES] = out.reshape(per, rows, LANES)

    def wide_row(k, s):
        cf = coef[k, pl.ds(s, 1), :]
        return jnp.concatenate([cf] * num_groups, axis=1)

    def fold(val):
        acc = val[:, :LANES]
        for g in range(1, num_groups):
            acc = acc + val[:, g * LANES : (g + 1) * LANES]
        return jnp.sum(acc, axis=0, keepdims=True)

    def forward(t):
        @pl.when(me < sections - 1)
        def _():
            conv(wf, send_img, t)

    def send_images(j, c):
        t = j * CHUNKS + c
        if not relayed or j < last:
            each_copy(t, True, 0, start_copy)
            return

        @pl.when(me != low)
        def _():
            each_copy(t, True, 0, start_copy)

        def late(spot):
            relay_in(spot, True).start()
            img_copy(spot, direct).start()

        @pl.when(near(me == low, c > 0))
        def _():
            late(t - 1)

        @pl.when(near(me == low, c == CHUNKS - 1))
        def _():
            late(t)

    def recur(ref, val, j, t, s):
        val = val * wide_row(1, s) + ref[t - CHUNKS, s] * wide_row(2, s)
        if j > 1:
            val = val + ref[t - 2 * CHUNKS, s] * wide_row(3, s)
        return val

    def totals(j, c, count):
        slot = (j % 2) * CHUNKS + c
        for hop in range(1, sections):
            pk_copy(j, c, hop).wait()
        total = gath[slot, 0]
        for peer in range(1, sections):
            total = total + gath[slot, peer]
        total = jnp.broadcast_to(total, (per, LANES))
        outs = []
        for k in range(count):
            picked = jnp.where(lane_id == k * per + row_id, total, 0.0)
            outs.append(jnp.broadcast_to(jnp.sum(picked, axis=1, keepdims=True), (per, LANES)))
        return outs

    def rates(j, c):
        t = j * CHUNKS + c
        bias_c = spread_row(bias, c)
        sums = totals(j, c, 4 if j == 0 else 3)
        lead_now = lead_b[t]
        image_lead = bias_c * lead_now + 0.5 * sums[0]
        if j == 0:
            factor = 1.0 / jnp.sqrt(lead_now * lead_now + sums[3])
            fac_b[c] = factor
            alpha = factor * factor * (lead_now * image_lead + sums[1])
            lead_now = lead_now * factor
            image_lead = image_lead * factor
            power = factor * factor * sums[2]
            rest_lead = image_lead - alpha * lead_now
            beta = jnp.sqrt(image_lead * image_lead + power - alpha * alpha + 1e-06)
            lead_b[t] = lead_now
            inv = 1.0 / beta
            coef[1] = inv * factor
            coef[2] = -alpha * inv * factor
        else:
            beta_old = beta_b[t - CHUNKS]
            lead_old = lead_b[t - CHUNKS]
            alpha = lead_now * image_lead + sums[1]
            rest_lead = image_lead - alpha * lead_now - beta_old * lead_old
            beta = jnp.sqrt(image_lead * image_lead + sums[2] - alpha * alpha - beta_old * beta_old + 1e-06)
            inv = 1.0 / beta
            coef[1] = inv
            coef[2] = -alpha * inv
            coef[3] = -beta_old * inv * (fac_b[c] if j == 1 else 1.0)
        lead_b[t + CHUNKS] = rest_lead * inv
        alpha_b[t] = alpha
        beta_b[t] = beta

    def apply(j, c):
        t = j * CHUNKS + c
        final_step = j == last
        if not final_step:
            each_copy(t, False, 1, await_recv)

            @pl.when(me < sections - 1)
            def _():
                def shift_one(s, carry):
                    put_shifted(s, rec[t, s])
                    return carry

                lax.fori_loop(0, per, shift_one, 0)
                conv(wb, back, t)

            @pl.when(me == sections - 1)
            def _():
                back[t] = jnp.zeros((per, rows, width), jnp.float32)

        if j > 0:
            rates(j - 1, c)
        else:
            load(2, c).wait()
        coef[0] = lead_b[t]
        def early(s, carry):
            zs = recur(z, w_buf[c, s], j, t, s)
            z[t, s] = zs
            lin = table[labels[c * per + s]]
            part[0, pl.ds(s, 1), :] = fold(lin * zs)
            w = diag[c, s] * zs + lin * (0.5 * wide_row(0, s))
            part[1, pl.ds(s, 1), :] = fold(zs * w)
            return carry

        def closing_one(s, carry):
            image = recur(img, img[t, s], j, t, s)
            img[t, s] = image
            part[1, pl.ds(s, 1), :] -= fold(z[t, s] * (coup[c, s] * image))
            return carry

        if final_step:
            lax.fori_loop(0, per, early, 0)
        each_copy(t, True, 1, await_recv)

        @pl.when(me == 0)
        def _():
            img[t] = jnp.zeros((per, rows, width), jnp.float32)

        def one(s, carry):
            if j > 0:
                zs = recur(z, w_buf[c, s], j, t, s)
                z[t, s] = zs
                image = recur(img, img[t, s], j, t, s)
                img[t, s] = image
            else:
                zs = z[t, s]
                image = img[t, s]
            lin = table[labels[c * per + s]]
            pulled = back[t, s]
            if j > 0:
                pulled = recur(back, pulled, j, t, s)
                if j + 1 < last:
                    back[t, s] = pulled
            w = diag[c, s] * zs - 0.5 * (coup[c, s] * image + pulled)
            w = w + lin * (0.5 * wide_row(0, s))
            part[0, pl.ds(s, 1), :] = fold(lin * zs)
            part[1, pl.ds(s, 1), :] = fold(zs * w)
            w_buf[c, s] = w
            put_shifted(s, w)
            if j + 1 < last:
                send_scl[t + CHUNKS, s] = coup[c, s] * w
            part[2, pl.ds(s, 1), :] = fold(w * w)
            if j == 0:
                part[3, pl.ds(s, 1), :] = fold(zs * zs)
            return carry

        lax.fori_loop(0, per, closing_one if final_step else one, 0)
        if j + 1 < last:
            each_copy(t + CHUNKS, False, 0, start_copy)
        packet = jnp.zeros((per, LANES), jnp.float32)
        for k in range(4 if j == 0 else (2 if final_step else 3)):
            packet = jnp.where(lane_id == k * per + row_id, jnp.sum(part[k], axis=1, keepdims=True), packet)
        packet = jnp.sum(packet, axis=0, keepdims=True)
        slot = (j % 2) * CHUNKS + c
        pk[slot] = packet
        gath[slot, me] = packet
        for hop in range(1, sections):
            pk_copy(j, c, hop).start()

    def finish(c):
        t = last * CHUNKS + c
        bias_c = spread_row(bias, c)
        sums = totals(last, c, 2)
        lead_now = lead_b[t]
        alpha = lead_now * (bias_c * lead_now + 0.5 * sums[0]) + sums[1]
        alphas = [alpha_b[j * CHUNKS + c] for j in range(last)] + [alpha]
        betas = [beta_b[j * CHUNKS + c] for j in range(last)]
        n = ITERS
        zero = jnp.zeros((per, LANES), jnp.float32)
        tri = [[zero] * n for _ in range(n)]
        norm = zero
        for i in range(n):
            tri[i][i] = alphas[i]
            norm = norm + alphas[i] * alphas[i]
            if i + 1 < n:
                tri[i][i + 1] = betas[i]
                tri[i + 1][i] = betas[i]
                norm = norm + 2.0 * (betas[i] * betas[i])
        scale = 0.5 / jnp.sqrt(norm)
        sx = [[tri[i][k] * scale for k in range(n)] for i in range(n)]
        expo = [[zero + (1.0 if i == k else 0.0) for k in range(n)] for i in range(n)]
        for degree in range(12, 0, -1):
            nxt = []
            for i in range(n):
                line = []
                for k in range(n):
                    acc = None
                    for m in range(max(0, i - 1), min(n, i + 2)):
                        term = sx[i][m] * expo[m][k]
                        acc = term if acc is None else acc + term
                    acc = acc * (1.0 / degree)
                    line.append(acc + 1.0 if i == k else acc)
                nxt.append(line)
            expo = nxt
        for _ in range(4):
            nxt = [[None] * n for _ in range(n)]
            for i in range(n):
                for k in range(n):
                    acc = expo[i][0] * expo[0][k]
                    for m in range(1, n):
                        acc = acc + expo[i][m] * expo[m][k]
                    nxt[i][k] = acc
            expo = nxt
        trace = expo[0][0] + expo[1][1] + expo[2][2] + expo[3][3]
        inv = 1.0 / trace
        wt = [[expo[i][k] * inv for k in range(n)] for i in range(n)]
        soft = zero
        gbias = zero
        leads = [lead_b[i * CHUNKS + c] for i in range(n)]
        for i in range(n):
            for k in range(n):
                if abs(i - k) <= 1:
                    soft = soft + wt[i][k] * tri[i][k]
                gbias = gbias + wt[i][k] * (leads[i] * leads[k])
        mine = lane_id == c * per + row_id
        for k, val in enumerate((gbias, soft)):
            small[k : k + 1, :] += jnp.sum(jnp.where(mine, val, 0.0), axis=0, keepdims=True)
        fac = fac_b[c]

        def scaled_by(val, *which):
            for i in which:
                if i == 0:
                    val = val * fac
            return val

        for i in range(n):
            for k in range(n):
                coef[4 + i * n + k] = unit_count * scaled_by(wt[i][k], i, k)
        for k in range(n):
            val = wt[0][k] * leads[0]
            for i in range(1, n):
                val = val + wt[i][k] * leads[i]
            coef[4 + n * n + k] = math.sqrt(unit_count) * scaled_by(val, k)

        def final(s, carry):
            cf = [coef[4 + k, pl.ds(s, 1), :] for k in range(n * n + n)]
            for g in range(num_groups):
                cols = slice(g * LANES, (g + 1) * LANES)
                zs = [z[i * CHUNKS + c, s, :, cols] for i in range(n)]
                ims = [img[i * CHUNKS + c, s, :, cols] for i in range(n)]
                gd = gc = gl = None
                for k in range(n):
                    mixed = zs[0] * cf[k]
                    for i in range(1, n):
                        mixed = mixed + zs[i] * cf[i * n + k]
                    lin = zs[k] * cf[n * n + k]
                    if k == 0:
                        gd, gc, gl = zs[k] * mixed, -(ims[k] * mixed), lin
                    else:
                        gd, gc, gl = gd + zs[k] * mixed, gc - ims[k] * mixed, gl + lin
                grad_diag[c, s, :, cols] = gd
                grad_coup[c, s, :, cols] = gc
                grad_lin[c, s, :, cols] = gl
            return carry

        lax.fori_loop(0, per, final, 0)

    def begin(c, carry):
        load(0, c).wait()
        load(1, c).wait()

        def first(s, carry):
            val = z[c, s]
            send_scl[c, s] = coup[c, s] * val
            put_shifted(s, val)
            return carry

        lax.fori_loop(0, per, first, 0)

        @pl.when(me < sections - 1)
        def _():
            conv(wf, send_img, c)

        @pl.when(c == 0)
        def _():
            pl.semaphore_wait(barrier, sections - 1)

        each_copy(c, False, 0, start_copy)
        each_copy(c, True, 0, start_copy)
        return carry

    small[...] = jnp.zeros((2, LANES), jnp.float32)
    lax.fori_loop(0, CHUNKS, begin, 0)
    for tap_row in range(3):
        lay_out([jnp.transpose(kern[2 - tap_row, 2 - tap]) for tap in range(3)], wb, tap_row)
    load_table().wait()
    for which in range(3):
        load_row(which).wait()

    def spread_lead(c, carry):
        lead_b[c] = spread_row(lead0, c)
        return carry

    lax.fori_loop(0, CHUNKS, spread_lead, 0)

    def pass_first(c, carry):
        pass_on(c, True)
        return carry

    lax.fori_loop(0, CHUNKS, pass_first, 0)

    for j in range(last):

        def step(c, carry):
            ahead = 1 if j + 1 < last else 2

            @pl.when(c >= ahead)
            def _():
                pass_on((j + 1) * CHUNKS + c - ahead, j + 1 < last)

            if j > 0:

                @pl.when(c == 0)
                def _():
                    pass_on((j + 1) * CHUNKS - 1, True)

            apply(j, c)
            forward((j + 1) * CHUNKS + c)
            send_images(j + 1, c)
            return carry

        lax.fori_loop(0, CHUNKS, step, 0)

    pass_on(ITERS * CHUNKS - 2, False)
    pass_on(ITERS * CHUNKS - 1, False)

    def settle(t, carry):
        each_copy(t, True, 0, await_send)
        if relayed:

            @pl.when(me == img_via)
            def _():
                relay_out(t, True).wait_send()

        return carry

    def settle_scaled(t, carry):
        each_copy(t, False, 0, await_send)
        if relayed:

            @pl.when(me == scl_via)
            def _():
                relay_out(t, False).wait_send()

        return carry

    def closing(c, carry):
        for j in range(last):
            settle(j * CHUNKS + c, 0)
            settle_scaled(j * CHUNKS + c, 0)
        apply(last, c)
        return carry

    def ending(c, carry):
        finish(c)
        return carry

    lax.fori_loop(0, CHUNKS, closing, 0)
    lax.fori_loop(last * CHUNKS, ITERS * CHUNKS, settle, 0)
    lax.fori_loop(0, CHUNKS, ending, 0)


def hand_over(in_d, in_c, in_l, small, out_d, out_c, out_l, gbias, soft, sums, row_b, row_s, sems):
    moves = [
        pltpu.make_async_copy(src, dst, sems.at[which])
        for which, (src, dst) in enumerate(((in_d, out_d), (in_c, out_c), (in_l, out_l)))
    ]
    fetch = pltpu.make_async_copy(small, sums, sems.at[3])
    fetch.start()
    for move in moves:
        move.start()
    fetch.wait()
    count = gbias.shape[0]
    row_b[...] = sums[0, :count]
    row_s[...] = sums[1, :count]
    rows = [pltpu.make_async_copy(row_b, gbias, sems.at[4]), pltpu.make_async_copy(row_s, soft, sems.at[5])]
    for row in rows:
        row.start()
    for move in moves + rows:
        move.wait()


def in_hbm(array):
    return pltpu.with_memory_space_constraint(array, pltpu.HBM)


def body(start_lead, start_field, diag_dual, coupling_dual, linear_table, labels, bias_dual, kernels):
    sections = lax.axis_size("layer")
    specs, _, rows, width = start_field.shape
    unit_count = sections * rows * width
    per = specs // CHUNKS
    chan = kernels.shape[-1]
    block = (per, rows, width)
    shape = (CHUNKS,) + block
    full = pl.BlockSpec(memory_space=pltpu.VMEM)
    anywhere = pl.BlockSpec(memory_space=pl.ANY)
    f32, bf16 = jnp.float32, jnp.bfloat16
    dma = pltpu.SemaphoreType.DMA
    slots, sent = ITERS * CHUNKS, (ITERS - 1) * CHUNKS
    small_block = (per, LANES)
    outs = pl.pallas_call(
        functools.partial(kernel_body, sections, float(unit_count)),
        out_shape=[pltpu.VMEM(shape, f32)] * 3 + [pltpu.VMEM((2, LANES), f32)],
        in_specs=[anywhere] * 8,
        out_specs=[full] * 4,
        scratch_shapes=[
            pltpu.VMEM((slots,) + block, f32),
            pltpu.VMEM((slots,) + block, f32),
            pltpu.VMEM((sent,) + block, f32),
            pltpu.VMEM((slots,) + block, f32),
            pltpu.VMEM((sent,) + block, f32),
            pltpu.VMEM(shape, f32),
            pltpu.VMEM((sent,) + block, f32),
            pltpu.VMEM((per * rows, width + LANES), bf16),
            pltpu.VMEM((per * rows, width + LANES), bf16),
            pltpu.VMEM((4 * chan, 12 * chan), bf16),
            pltpu.VMEM((4 * chan, 12 * chan), bf16),
            pltpu.VMEM((4,) + small_block, f32),
            pltpu.VMEM((24,) + small_block, f32),
            pltpu.VMEM((slots,) + small_block, f32),
            pltpu.VMEM((slots,) + small_block, f32),
            pltpu.VMEM((slots,) + small_block, f32),
            pltpu.VMEM((CHUNKS,) + small_block, f32),
            pltpu.VMEM((2 * CHUNKS, 1, LANES), f32),
            pltpu.VMEM((2 * CHUNKS, sections, 1, LANES), f32),
            pltpu.VMEM((slots, per - per // 2, rows, width), f32),
            pltpu.VMEM(shape, f32),
            pltpu.VMEM(shape, f32),
            pltpu.VMEM((linear_table.shape[0], rows, width), f32),
            pltpu.VMEM(kernels.shape[1:], f32),
            dma((slots,)),
            dma((slots,)),
            dma((sent,)),
            dma((sent,)),
            dma((2 * CHUNKS, sections)),
            dma((2 * CHUNKS, sections)),
            dma((slots,)),
            dma((slots,)),
            dma((slots,)),
            dma((slots,)),
            pltpu.SMEM((specs,), jnp.int32),
            pltpu.SMEM((specs,), f32),
            pltpu.SMEM((specs,), f32),
            dma((3, CHUNKS)),
            dma((5,)),
        ],
        compiler_params=pltpu.CompilerParams(collective_id=0, has_side_effects=True, vmem_limit_bytes=44 * 1024 * 1024),
    )(
        in_hbm(labels),
        in_hbm(start_lead),
        in_hbm(bias_dual),
        in_hbm(start_field.reshape(shape)),
        in_hbm(diag_dual.reshape(shape)),
        in_hbm(coupling_dual.reshape(shape)),
        in_hbm(linear_table.reshape(linear_table.shape[0], rows, width)),
        in_hbm(kernels.reshape(kernels.shape[1:])),
    )
    done = pl.pallas_call(
        hand_over,
        out_shape=[jax.ShapeDtypeStruct(shape, f32)] * 3 + [jax.ShapeDtypeStruct((specs,), f32)] * 2,
        in_specs=[anywhere] * 4,
        out_specs=[anywhere] * 5,
        scratch_shapes=[pltpu.VMEM((2, LANES), f32), pltpu.VMEM((specs,), f32), pltpu.VMEM((specs,), f32), dma((6,))],
        compiler_params=pltpu.CompilerParams(vmem_limit_bytes=8 * 1024 * 1024),
    )(*outs)
    big = [out.reshape(start_field.shape) for out in done[:3]]
    return (*big, done[3], done[4])


def solution(mesh):
    placed = (
        P("spec"),
        P("spec", "layer", None, None),
        P("spec", "layer", None, None),
        P("spec", "layer", None, None),
        P(None, "layer", None, None),
        P("spec"),
        P("spec"),
        P("layer", None, None, None, None),
    )
    return jax.shard_map(
        body,
        mesh=mesh,
        in_specs=placed,
        out_specs=(
            P("spec", "layer", None, None),
            P("spec", "layer", None, None),
            P("spec", "layer", None, None),
            P("spec"),
            P("spec"),
        ),
        check_vma=False,
    )
```

```python
import functools
import math

import jax
import jax.numpy as jnp
from jax import lax
from jax.experimental import pallas as pl
from jax.experimental.pallas import tpu as pltpu
from jax.sharding import PartitionSpec as P

ITERS = 4
CHUNKS = 4
LANES = 128
RELAY_SECTIONS = 8
MESH = pl.DeviceIdType.MESH


def gradients(cf, num_groups, parts, put):
    n = ITERS
    for g in range(num_groups):
        cols = slice(g * LANES, (g + 1) * LANES)
        zs, ims = parts(cols)
        gd = gc = gl = None
        for k in range(n):
            mixed = zs[0] * cf[k]
            for i in range(1, n):
                mixed = mixed + zs[i] * cf[i * n + k]
            lin = zs[k] * cf[n * n + k]
            if k == 0:
                gd, gc, gl = zs[k] * mixed, -(ims[k] * mixed), lin
            else:
                gd, gc, gl = gd + zs[k] * mixed, gc - ims[k] * mixed, gl + lin
        put(cols, (gd, gc, gl))


def mixing(alphas, betas, leads, fac, unit_count, coef, base):
    n = ITERS
    zero = jnp.zeros_like(alphas[0])
    tri = [[zero] * n for _ in range(n)]
    norm = zero
    for i in range(n):
        tri[i][i] = alphas[i]
        norm = norm + alphas[i] * alphas[i]
        if i + 1 < n:
            tri[i][i + 1] = betas[i]
            tri[i + 1][i] = betas[i]
            norm = norm + 2.0 * (betas[i] * betas[i])
    scale = 0.5 / jnp.sqrt(norm)
    sx = [[tri[i][k] * scale for k in range(n)] for i in range(n)]
    expo = [[zero + (1.0 if i == k else 0.0) for k in range(n)] for i in range(n)]
    for degree in range(12, 0, -1):
        nxt = []
        for i in range(n):
            line = []
            for k in range(n):
                acc = None
                for m in range(max(0, i - 1), min(n, i + 2)):
                    term = sx[i][m] * expo[m][k]
                    acc = term if acc is None else acc + term
                acc = acc * (1.0 / degree)
                line.append(acc + 1.0 if i == k else acc)
            nxt.append(line)
        expo = nxt
    for _ in range(4):
        nxt = [[None] * n for _ in range(n)]
        for i in range(n):
            for k in range(n):
                acc = expo[i][0] * expo[0][k]
                for m in range(1, n):
                    acc = acc + expo[i][m] * expo[m][k]
                nxt[i][k] = acc
        expo = nxt
    trace = expo[0][0] + expo[1][1] + expo[2][2] + expo[3][3]
    inv = 1.0 / trace
    wt = [[expo[i][k] * inv for k in range(n)] for i in range(n)]
    soft = zero
    gbias = zero
    for i in range(n):
        for k in range(n):
            if abs(i - k) <= 1:
                soft = soft + wt[i][k] * tri[i][k]
            gbias = gbias + wt[i][k] * (leads[i] * leads[k])

    def scaled_by(val, *which):
        for i in which:
            if i == 0:
                val = val * fac
        return val

    for i in range(n):
        for k in range(n):
            coef[base + i * n + k] = unit_count * scaled_by(wt[i][k], i, k)
    for k in range(n):
        val = wt[0][k] * leads[0]
        for i in range(1, n):
            val = val + wt[i][k] * leads[i]
        coef[base + n * n + k] = math.sqrt(unit_count) * scaled_by(val, k)
    return gbias, soft


def kernel_body(
    sections,
    unit_count,
    labels_hbm,
    lead0_hbm,
    bias_hbm,
    start_hbm,
    diag_hbm,
    coup_hbm,
    table_hbm,
    kern_hbm,
    grad_diag,
    grad_coup,
    grad_lin,
    small,
    last_z,
    last_img,
    last_coef,
    z,
    img,
    rec,
    send_img,
    send_scl,
    w_buf,
    back,
    xh,
    xl,
    wf,
    wb,
    part,
    coef,
    lead_b,
    alpha_b,
    beta_b,
    fac_b,
    pk,
    gath,
    rly,
    diag,
    coup,
    table,
    kern,
    s_img_s,
    s_img_r,
    s_scl_s,
    s_scl_r,
    s_pk_s,
    s_pk_r,
    s_in_s,
    s_in_r,
    s_out_s,
    s_out_r,
    labels,
    lead0,
    bias,
    s_load,
    s_one,
    s_keep,
):
    me = lax.axis_index("layer")
    per, rows, width = z.shape[1:]
    num_groups = width // LANES
    half = LANES // 2
    block_rows = per * rows
    last = ITERS - 1

    barrier = pltpu.get_barrier_semaphore()
    for hop in range(1, sections):
        peer = lax.rem(me + hop, sections)
        pl.semaphore_signal(barrier, inc=1, device_id={"layer": peer}, device_id_type=MESH)

    def load_kern():
        return pltpu.make_async_copy(kern_hbm, kern, s_one.at[0])

    def load_table():
        return pltpu.make_async_copy(table_hbm, table, s_one.at[1])

    def load(which, c):
        src, dst = ((start_hbm, z), (coup_hbm, coup), (diag_hbm, diag))[which]
        return pltpu.make_async_copy(src.at[c], dst.at[c], s_load.at[which, c])

    def load_row(which):
        src, dst = ((lead0_hbm, lead0), (labels_hbm, labels), (bias_hbm, bias))[which]
        return pltpu.make_async_copy(src, dst, s_one.at[2 + which])

    load_kern().start()
    for c in range(CHUNKS):
        load(0, c).start()
        load(1, c).start()
    for which in range(3):
        load_row(which).start()
    load_table().start()
    for c in range(CHUNKS):
        load(2, c).start()

    load_kern().wait()
    chan = kern.shape[-1]
    zero_tap = jnp.zeros((chan, chan), jnp.float32)

    def lay_out(taps, out, tap_row):
        for in_pos in range(4):
            pieces = [taps[in_pos - q] if 0 <= in_pos - q <= 2 else zero_tap for q in range(2)]
            val = jnp.concatenate(pieces, axis=1)
            top = val.astype(jnp.bfloat16)
            at = slice(in_pos * chan, (in_pos + 1) * chan)
            out[at, tap_row * LANES : (tap_row + 1) * LANES] = top
            out[at, (3 + tap_row) * LANES : (4 + tap_row) * LANES] = (val - top.astype(jnp.float32)).astype(jnp.bfloat16)

    for tap_row in range(3):
        lay_out([kern[tap_row, tap] for tap in range(3)], wf, tap_row)

    relayed = sections == RELAY_SECTIONS
    low, high = sections // 2 - 1, sections // 2
    img_via, scl_via = sections - 1, 0
    direct = per // 2
    near = jnp.logical_and

    def relay_in(t, images):
        src = send_img if images else send_scl
        return pltpu.make_async_remote_copy(
            src_ref=src.at[t, pl.ds(direct, per - direct)],
            dst_ref=rly.at[t],
            send_sem=s_in_s.at[t],
            recv_sem=s_in_r.at[t],
            device_id={"layer": jnp.int32(img_via if images else scl_via)},
            device_id_type=MESH,
        )

    def relay_out(t, images):
        dst = img if images else rec
        return pltpu.make_async_remote_copy(
            src_ref=rly.at[t],
            dst_ref=dst.at[t, pl.ds(direct, per - direct)],
            send_sem=s_out_s.at[t],
            recv_sem=s_out_r.at[t],
            device_id={"layer": jnp.int32(high if images else low)},
            device_id_type=MESH,
        )

    def pass_on(t, scaled_too):
        if not relayed:
            return
        for images, via in ((False, scl_via), (True, img_via)):
            if images or scaled_too:

                @pl.when(me == via)
                def _():
                    relay_in(t, images).wait_recv()
                    relay_out(t, images).start()

    def img_copy(t, count=per):
        return pltpu.make_async_remote_copy(
            src_ref=send_img.at[t, pl.ds(0, count)],
            dst_ref=img.at[t, pl.ds(0, count)],
            send_sem=s_img_s.at[t],
            recv_sem=s_img_r.at[t],
            device_id={"layer": lax.rem(me + 1, sections)},
            device_id_type=MESH,
        )

    def scl_copy(t, count=per):
        return pltpu.make_async_remote_copy(
            src_ref=send_scl.at[t, pl.ds(0, count)],
            dst_ref=rec.at[t, pl.ds(0, count)],
            send_sem=s_scl_s.at[t],
            recv_sem=s_scl_r.at[t],
            device_id={"layer": lax.rem(me + sections - 1, sections)},
            device_id_type=MESH,
        )

    def each_copy(t, images, side, act):
        copy = img_copy if images else scl_copy
        if images:
            has = me < sections - 1 if side == 0 else me > 0
            middle = low if side == 0 else high
        else:
            has = me > 0 if side == 0 else me < sections - 1
            middle = high if side == 0 else low
        if not relayed:

            @pl.when(has)
            def _():
                act(copy(t))

            return

        @pl.when(near(has, me != middle))
        def _():
            act(copy(t))

        @pl.when(me == middle)
        def _():
            act(relay_in(t, images) if side == 0 else relay_out(t, images))
            act(copy(t, direct))

    def pk_copy(j, c, hop):
        slot = (j % 2) * CHUNKS + c
        return pltpu.make_async_remote_copy(
            src_ref=pk.at[slot],
            dst_ref=gath.at[slot, me],
            send_sem=s_pk_s.at[slot, hop],
            recv_sem=s_pk_r.at[slot, hop],
            device_id={"layer": lax.rem(me + hop, sections)},
            device_id_type=MESH,
        )

    def start_copy(copy):
        copy.start()

    def await_recv(copy):
        copy.wait_recv()

    def await_send(copy):
        copy.wait_send()

    row_id = lax.broadcasted_iota(jnp.int32, (per, LANES), 0)
    lane_id = lax.broadcasted_iota(jnp.int32, (per, LANES), 1)

    def spread_row(values, c):
        out = jnp.zeros((per, LANES), jnp.float32)
        for s in range(per):
            out = jnp.where(row_id == s, values[c * per + s], out)
        return out

    def put_shifted(s, val):
        wide = jnp.concatenate([val, jnp.zeros((rows, LANES), jnp.float32)], axis=1)
        wide = pltpu.roll(wide, half, 1)
        top = wide.astype(jnp.bfloat16)
        at = pl.ds(pl.multiple_of(s * rows, rows), rows)
        xh[at, :] = top
        xl[at, :] = (wide - top.astype(jnp.float32)).astype(jnp.bfloat16)

    def conv(wts, out_ref, t):
        row = lax.rem(lax.broadcasted_iota(jnp.int32, (block_rows, LANES), 0), rows)
        cols = [slice(g * LANES, (g + 2) * LANES) for g in range(num_groups)]
        a_hi = jnp.concatenate([xh[:, at] for at in cols], axis=0)
        a_lo = jnp.concatenate([xl[:, at] for at in cols], axis=0)
        both = jnp.dot(a_hi, wts[...], preferred_element_type=jnp.float32)
        prod = both[:, : 3 * LANES] + both[:, 3 * LANES :]
        prod += jnp.dot(a_lo, wts[:, : 3 * LANES], preferred_element_type=jnp.float32)
        for g in range(num_groups):
            mine = prod[g * block_rows : (g + 1) * block_rows]
            above = pltpu.roll(mine[:, :LANES], 1, 0)
            below = pltpu.roll(mine[:, 2 * LANES :], block_rows - 1, 0)
            out = mine[:, LANES : 2 * LANES]
            out += jnp.where(row == 0, 0.0, above)
            out += jnp.where(row == rows - 1, 0.0, below)
            out_ref[t, :, :, g * LANES : (g + 1) * LANES] = out.reshape(per, rows, LANES)

    def wide_row(k, s):
        cf = coef[k, pl.ds(s, 1), :]
        return jnp.concatenate([cf] * num_groups, axis=1)

    def fold(val):
        acc = val[:, :LANES]
        for g in range(1, num_groups):
            acc = acc + val[:, g * LANES : (g + 1) * LANES]
        return jnp.sum(acc, axis=0, keepdims=True)

    def forward(t):
        @pl.when(me < sections - 1)
        def _():
            conv(wf, send_img, t)

    def send_images(j, c):
        t = j * CHUNKS + c
        if not relayed or j < last:
            each_copy(t, True, 0, start_copy)
            return

        @pl.when(me != low)
        def _():
            each_copy(t, True, 0, start_copy)

        def late(spot):
            relay_in(spot, True).start()
            img_copy(spot, direct).start()

        @pl.when(near(me == low, c > 0))
        def _():
            late(t - 1)

        @pl.when(near(me == low, c == CHUNKS - 1))
        def _():
            late(t)

    def recur(ref, val, j, t, s):
        val = val * wide_row(1, s) + ref[t - CHUNKS, s] * wide_row(2, s)
        if j > 1:
            val = val + ref[t - 2 * CHUNKS, s] * wide_row(3, s)
        return val

    def totals(j, c, count):
        slot = (j % 2) * CHUNKS + c
        for hop in range(1, sections):
            pk_copy(j, c, hop).wait()
        total = gath[slot, 0]
        for peer in range(1, sections):
            total = total + gath[slot, peer]
        total = jnp.broadcast_to(total, (per, LANES))
        outs = []
        for k in range(count):
            picked = jnp.where(lane_id == k * per + row_id, total, 0.0)
            outs.append(jnp.broadcast_to(jnp.sum(picked, axis=1, keepdims=True), (per, LANES)))
        return outs

    def rates(j, c):
        t = j * CHUNKS + c
        bias_c = spread_row(bias, c)
        sums = totals(j, c, 4 if j == 0 else 3)
        lead_now = lead_b[t]
        image_lead = bias_c * lead_now + 0.5 * sums[0]
        if j == 0:
            factor = 1.0 / jnp.sqrt(lead_now * lead_now + sums[3])
            fac_b[c] = factor
            alpha = factor * factor * (lead_now * image_lead + sums[1])
            lead_now = lead_now * factor
            image_lead = image_lead * factor
            power = factor * factor * sums[2]
            rest_lead = image_lead - alpha * lead_now
            beta = jnp.sqrt(image_lead * image_lead + power - alpha * alpha + 1e-06)
            lead_b[t] = lead_now
            inv = 1.0 / beta
            coef[1] = inv * factor
            coef[2] = -alpha * inv * factor
        else:
            beta_old = beta_b[t - CHUNKS]
            lead_old = lead_b[t - CHUNKS]
            alpha = lead_now * image_lead + sums[1]
            rest_lead = image_lead - alpha * lead_now - beta_old * lead_old
            beta = jnp.sqrt(image_lead * image_lead + sums[2] - alpha * alpha - beta_old * beta_old + 1e-06)
            inv = 1.0 / beta
            coef[1] = inv
            coef[2] = -alpha * inv
            coef[3] = -beta_old * inv * (fac_b[c] if j == 1 else 1.0)
        lead_b[t + CHUNKS] = rest_lead * inv
        alpha_b[t] = alpha
        beta_b[t] = beta

    def apply(j, c):
        t = j * CHUNKS + c
        final_step = j == last
        if not final_step:
            each_copy(t, False, 1, await_recv)

            @pl.when(me < sections - 1)
            def _():
                def shift_one(s, carry):
                    put_shifted(s, rec[t, s])
                    return carry

                lax.fori_loop(0, per, shift_one, 0)
                conv(wb, back, t)

            @pl.when(me == sections - 1)
            def _():
                back[t] = jnp.zeros((per, rows, width), jnp.float32)

        if j > 0:
            rates(j - 1, c)
        else:
            load(2, c).wait()
        coef[0] = lead_b[t]
        def early(s, carry):
            zs = recur(z, w_buf[c, s], j, t, s)
            z[t, s] = zs
            lin = table[labels[c * per + s]]
            part[0, pl.ds(s, 1), :] = fold(lin * zs)
            w = diag[c, s] * zs + lin * (0.5 * wide_row(0, s))
            part[1, pl.ds(s, 1), :] = fold(zs * w)
            return carry

        def closing_one(s, carry):
            image = recur(img, img[t, s], j, t, s)
            img[t, s] = image
            part[1, pl.ds(s, 1), :] -= fold(z[t, s] * (coup[c, s] * image))
            return carry

        if final_step:
            lax.fori_loop(0, per, early, 0)
        each_copy(t, True, 1, await_recv)

        @pl.when(me == 0)
        def _():
            img[t] = jnp.zeros((per, rows, width), jnp.float32)

        def one(s, carry):
            if j > 0:
                zs = recur(z, w_buf[c, s], j, t, s)
                z[t, s] = zs
                image = recur(img, img[t, s], j, t, s)
                img[t, s] = image
            else:
                zs = z[t, s]
                image = img[t, s]
            lin = table[labels[c * per + s]]
            pulled = back[t, s]
            if j > 0:
                pulled = recur(back, pulled, j, t, s)
                if j + 1 < last:
                    back[t, s] = pulled
            w = diag[c, s] * zs - 0.5 * (coup[c, s] * image + pulled)
            w = w + lin * (0.5 * wide_row(0, s))
            part[0, pl.ds(s, 1), :] = fold(lin * zs)
            part[1, pl.ds(s, 1), :] = fold(zs * w)
            w_buf[c, s] = w
            put_shifted(s, w)
            if j + 1 < last:
                send_scl[t + CHUNKS, s] = coup[c, s] * w
            part[2, pl.ds(s, 1), :] = fold(w * w)
            if j == 0:
                part[3, pl.ds(s, 1), :] = fold(zs * zs)
            return carry

        lax.fori_loop(0, per, closing_one if final_step else one, 0)
        if j + 1 < last:
            each_copy(t + CHUNKS, False, 0, start_copy)
        packet = jnp.zeros((per, LANES), jnp.float32)
        for k in range(4 if j == 0 else (2 if final_step else 3)):
            packet = jnp.where(lane_id == k * per + row_id, jnp.sum(part[k], axis=1, keepdims=True), packet)
        packet = jnp.sum(packet, axis=0, keepdims=True)
        slot = (j % 2) * CHUNKS + c
        pk[slot] = packet
        gath[slot, me] = packet
        for hop in range(1, sections):
            pk_copy(j, c, hop).start()

    def finish(c, with_grads):
        t = last * CHUNKS + c
        bias_c = spread_row(bias, c)
        sums = totals(last, c, 2)
        lead_now = lead_b[t]
        alpha = lead_now * (bias_c * lead_now + 0.5 * sums[0]) + sums[1]
        alphas = [alpha_b[j * CHUNKS + c] for j in range(last)] + [alpha]
        betas = [beta_b[j * CHUNKS + c] for j in range(last)]
        leads = [lead_b[j * CHUNKS + c] for j in range(ITERS)]
        if not with_grads:
            for k, val in enumerate(alphas + betas + leads + [fac_b[c]]):
                last_coef[k] = val
            return

        gbias, soft = mixing(alphas, betas, leads, fac_b[c], unit_count, coef, 4)
        mine = lane_id == c * per + row_id
        for k, val in enumerate((gbias, soft)):
            small[k : k + 1, :] += jnp.sum(jnp.where(mine, val, 0.0), axis=0, keepdims=True)
        n = ITERS

        def final(s, carry):
            cf = [coef[4 + k, pl.ds(s, 1), :] for k in range(n * n + n)]

            def parts(cols):
                return [[ref[i * CHUNKS + c, s, :, cols] for i in range(n)] for ref in (z, img)]

            def put(cols, values):
                for ref, val in zip((grad_diag, grad_coup, grad_lin), values):
                    ref[c, s, :, cols] = val

            gradients(cf, num_groups, parts, put)
            return carry

        lax.fori_loop(0, per, final, 0)

    def begin(c, carry):
        load(0, c).wait()
        load(1, c).wait()

        def first(s, carry):
            val = z[c, s]
            send_scl[c, s] = coup[c, s] * val
            put_shifted(s, val)
            return carry

        lax.fori_loop(0, per, first, 0)

        @pl.when(me < sections - 1)
        def _():
            conv(wf, send_img, c)

        @pl.when(c == 0)
        def _():
            pl.semaphore_wait(barrier, sections - 1)

        each_copy(c, False, 0, start_copy)
        each_copy(c, True, 0, start_copy)
        return carry

    small[...] = jnp.zeros((2, LANES), jnp.float32)
    lax.fori_loop(0, CHUNKS, begin, 0)
    for tap_row in range(3):
        lay_out([jnp.transpose(kern[2 - tap_row, 2 - tap]) for tap in range(3)], wb, tap_row)
    load_table().wait()
    for which in range(3):
        load_row(which).wait()

    def spread_lead(c, carry):
        lead_b[c] = spread_row(lead0, c)
        return carry

    lax.fori_loop(0, CHUNKS, spread_lead, 0)

    def pass_first(c, carry):
        pass_on(c, True)
        return carry

    lax.fori_loop(0, CHUNKS, pass_first, 0)

    for j in range(last):

        def step(c, carry):
            ahead = 1 if j + 1 < last else 2

            @pl.when(c >= ahead)
            def _():
                pass_on((j + 1) * CHUNKS + c - ahead, j + 1 < last)

            if j > 0:

                @pl.when(c == 0)
                def _():
                    pass_on((j + 1) * CHUNKS - 1, True)

            apply(j, c)
            forward((j + 1) * CHUNKS + c)
            send_images(j + 1, c)
            return carry

        lax.fori_loop(0, CHUNKS, step, 0)

    pass_on(ITERS * CHUNKS - 2, False)
    pass_on(ITERS * CHUNKS - 1, False)

    def settle(t, carry):
        each_copy(t, True, 0, await_send)
        if relayed:

            @pl.when(me == img_via)
            def _():
                relay_out(t, True).wait_send()

        return carry

    def settle_scaled(t, carry):
        each_copy(t, False, 0, await_send)
        if relayed:

            @pl.when(me == scl_via)
            def _():
                relay_out(t, False).wait_send()

        return carry

    def closing(c, carry):
        for j in range(last):
            settle(j * CHUNKS + c, 0)
            settle_scaled(j * CHUNKS + c, 0)
        apply(last, c)
        return carry

    def ending(c, carry):
        finish(c, True)
        return carry

    lax.fori_loop(0, CHUNKS, closing, 0)
    lax.fori_loop(last * CHUNKS, ITERS * CHUNKS, settle, 0)
    keeps = [
        pltpu.make_async_copy(src.at[j * CHUNKS + CHUNKS - 1], dst.at[j], s_keep.at[which, j])
        for which, (src, dst) in enumerate(((z, last_z), (img, last_img)))
        for j in range(ITERS)
    ]
    for keep in keeps:
        keep.start()
    lax.fori_loop(0, CHUNKS - 1, ending, 0)
    for keep in keeps:
        keep.wait()
    finish(CHUNKS - 1, False)


def hand_over(unit_count, in_d, in_c, in_l, small, zs, ims, known, out_d, out_c, out_l, gbias, soft, sums, row_b, row_s, new, coef, sems):
    pairs = ((in_d, out_d), (in_c, out_c), (in_l, out_l))
    old = pl.ds(0, CHUNKS - 1)
    fetch = pltpu.make_async_copy(small, sums, sems.at[8])
    fetch.start()
    moves = [pltpu.make_async_copy(src.at[old], dst.at[old], sems.at[which]) for which, (src, dst) in enumerate(pairs)]
    for move in moves:
        move.start()
    count = coef.shape[0]
    per, width = zs.shape[1], zs.shape[-1]
    n = ITERS
    rows_in = [known[k] for k in range(3 * n)]
    bias_part, soft_part = mixing(rows_in[:n], rows_in[n : 2 * n - 1], rows_in[2 * n - 1 : 3 * n - 1], rows_in[3 * n - 1], unit_count, coef, 0)

    def final(s, carry):
        cf = [coef[k, pl.ds(s, 1), :] for k in range(count)]

        def parts(cols):
            return [[ref[i, s, :, cols] for i in range(ITERS)] for ref in (zs, ims)]

        def put(cols, values):
            for which, val in enumerate(values):
                new[which, s, :, cols] = val

        gradients(cf, width // LANES, parts, put)
        return carry

    lax.fori_loop(0, per, final, 0)
    moves += [pltpu.make_async_copy(new.at[which], dst.at[CHUNKS - 1], sems.at[3 + which]) for which, (_, dst) in enumerate(pairs)]
    for move in moves[3:]:
        move.start()
    fetch.wait()
    specs = gbias.shape[0]
    lane = lax.broadcasted_iota(jnp.int32, (per, LANES), 1)
    mine = lane == (CHUNKS - 1) * per + lax.broadcasted_iota(jnp.int32, (per, LANES), 0)
    for k, (row, part) in enumerate(((row_b, bias_part), (row_s, soft_part))):
        whole = sums[k : k + 1, :] + jnp.sum(jnp.where(mine, part, 0.0), axis=0, keepdims=True)
        row[...] = whole[0, :specs]
    rows = [pltpu.make_async_copy(row_b, gbias, sems.at[6]), pltpu.make_async_copy(row_s, soft, sems.at[7])]
    for row in rows:
        row.start()
    for move in moves + rows:
        move.wait()


def in_hbm(array):
    return pltpu.with_memory_space_constraint(array, pltpu.HBM)


def body(start_lead, start_field, diag_dual, coupling_dual, linear_table, labels, bias_dual, kernels):
    sections = lax.axis_size("layer")
    specs, _, rows, width = start_field.shape
    unit_count = sections * rows * width
    per = specs // CHUNKS
    chan = kernels.shape[-1]
    block = (per, rows, width)
    shape = (CHUNKS,) + block
    full = pl.BlockSpec(memory_space=pltpu.VMEM)
    anywhere = pl.BlockSpec(memory_space=pl.ANY)
    f32, bf16 = jnp.float32, jnp.bfloat16
    dma = pltpu.SemaphoreType.DMA
    slots, sent = ITERS * CHUNKS, (ITERS - 1) * CHUNKS
    small_block = (per, LANES)
    outs = pl.pallas_call(
        functools.partial(kernel_body, sections, float(unit_count)),
        out_shape=[pltpu.VMEM(shape, f32)] * 3 + [pltpu.VMEM((2, LANES), f32)] + [pltpu.VMEM((ITERS,) + block, f32)] * 2 + [pltpu.VMEM((3 * ITERS,) + small_block, f32)],
        in_specs=[anywhere] * 8,
        out_specs=[full] * 7,
        scratch_shapes=[
            pltpu.VMEM((slots,) + block, f32),
            pltpu.VMEM((slots,) + block, f32),
            pltpu.VMEM((sent,) + block, f32),
            pltpu.VMEM((slots,) + block, f32),
            pltpu.VMEM((sent,) + block, f32),
            pltpu.VMEM(shape, f32),
            pltpu.VMEM((sent,) + block, f32),
            pltpu.VMEM((per * rows, width + LANES), bf16),
            pltpu.VMEM((per * rows, width + LANES), bf16),
            pltpu.VMEM((4 * chan, 12 * chan), bf16),
            pltpu.VMEM((4 * chan, 12 * chan), bf16),
            pltpu.VMEM((4,) + small_block, f32),
            pltpu.VMEM((24,) + small_block, f32),
            pltpu.VMEM((slots,) + small_block, f32),
            pltpu.VMEM((slots,) + small_block, f32),
            pltpu.VMEM((slots,) + small_block, f32),
            pltpu.VMEM((CHUNKS,) + small_block, f32),
            pltpu.VMEM((2 * CHUNKS, 1, LANES), f32),
            pltpu.VMEM((2 * CHUNKS, sections, 1, LANES), f32),
            pltpu.VMEM((slots, per - per // 2, rows, width), f32),
            pltpu.VMEM(shape, f32),
            pltpu.VMEM(shape, f32),
            pltpu.VMEM((linear_table.shape[0], rows, width), f32),
            pltpu.VMEM(kernels.shape[1:], f32),
            dma((slots,)),
            dma((slots,)),
            dma((sent,)),
            dma((sent,)),
            dma((2 * CHUNKS, sections)),
            dma((2 * CHUNKS, sections)),
            dma((slots,)),
            dma((slots,)),
            dma((slots,)),
            dma((slots,)),
            pltpu.SMEM((specs,), jnp.int32),
            pltpu.SMEM((specs,), f32),
            pltpu.SMEM((specs,), f32),
            dma((3, CHUNKS)),
            dma((5,)),
            dma((2, ITERS)),
        ],
        compiler_params=pltpu.CompilerParams(collective_id=0, has_side_effects=True, vmem_limit_bytes=44 * 1024 * 1024),
    )(
        in_hbm(labels),
        in_hbm(start_lead),
        in_hbm(bias_dual),
        in_hbm(start_field.reshape(shape)),
        in_hbm(diag_dual.reshape(shape)),
        in_hbm(coupling_dual.reshape(shape)),
        in_hbm(linear_table.reshape(linear_table.shape[0], rows, width)),
        in_hbm(kernels.reshape(kernels.shape[1:])),
    )
    done = pl.pallas_call(
        functools.partial(hand_over, float(unit_count)),
        out_shape=[jax.ShapeDtypeStruct(shape, f32)] * 3 + [jax.ShapeDtypeStruct((specs,), f32)] * 2,
        in_specs=[anywhere] * 4 + [full] * 3,
        out_specs=[anywhere] * 5,
        scratch_shapes=[pltpu.VMEM((2, LANES), f32), pltpu.VMEM((specs,), f32), pltpu.VMEM((specs,), f32), pltpu.VMEM((3,) + block, f32), pltpu.VMEM((20,) + small_block, f32), dma((9,))],
        compiler_params=pltpu.CompilerParams(vmem_limit_bytes=8 * 1024 * 1024),
    )(*outs)
    big = [out.reshape(start_field.shape) for out in done[:3]]
    return (*big, done[3], done[4])


def solution(mesh):
    placed = (
        P("spec"),
        P("spec", "layer", None, None),
        P("spec", "layer", None, None),
        P("spec", "layer", None, None),
        P(None, "layer", None, None),
        P("spec"),
        P("spec"),
        P("layer", None, None, None, None),
    )
    return jax.shard_map(
        body,
        mesh=mesh,
        in_specs=placed,
        out_specs=(
            P("spec", "layer", None, None),
            P("spec", "layer", None, None),
            P("spec", "layer", None, None),
            P("spec"),
            P("spec"),
        ),
        check_vma=False,
    )
```

```python
import functools
import math

import jax
import jax.numpy as jnp
from jax import lax
from jax.experimental import pallas as pl
from jax.experimental.pallas import tpu as pltpu
from jax.sharding import PartitionSpec as P

ITERS = 4
CHUNKS = 4
LANES = 128
RELAY_SECTIONS = 8
MESH = pl.DeviceIdType.MESH


def gradients(cf, num_groups, parts, put):
    n = ITERS
    for g in range(num_groups):
        cols = slice(g * LANES, (g + 1) * LANES)
        zs, ims = parts(cols)
        gd = gc = gl = None
        for k in range(n):
            mixed = zs[0] * cf[k]
            for i in range(1, n):
                mixed = mixed + zs[i] * cf[i * n + k]
            lin = zs[k] * cf[n * n + k]
            if k == 0:
                gd, gc, gl = zs[k] * mixed, -(ims[k] * mixed), lin
            else:
                gd, gc, gl = gd + zs[k] * mixed, gc - ims[k] * mixed, gl + lin
        put(cols, (gd, gc, gl))


def mixing(alphas, betas, leads, fac, unit_count, coef, base):
    n = ITERS
    zero = jnp.zeros_like(alphas[0])
    tri = [[zero] * n for _ in range(n)]
    norm = zero
    for i in range(n):
        tri[i][i] = alphas[i]
        norm = norm + alphas[i] * alphas[i]
        if i + 1 < n:
            tri[i][i + 1] = betas[i]
            tri[i + 1][i] = betas[i]
            norm = norm + 2.0 * (betas[i] * betas[i])
    scale = 0.5 / jnp.sqrt(norm)
    sx = [[tri[i][k] * scale for k in range(n)] for i in range(n)]
    expo = [[zero + (1.0 if i == k else 0.0) for k in range(n)] for i in range(n)]
    for degree in range(12, 0, -1):
        nxt = []
        for i in range(n):
            line = []
            for k in range(n):
                acc = None
                for m in range(max(0, i - 1), min(n, i + 2)):
                    term = sx[i][m] * expo[m][k]
                    acc = term if acc is None else acc + term
                acc = acc * (1.0 / degree)
                line.append(acc + 1.0 if i == k else acc)
            nxt.append(line)
        expo = nxt
    for _ in range(4):
        nxt = [[None] * n for _ in range(n)]
        for i in range(n):
            for k in range(n):
                acc = expo[i][0] * expo[0][k]
                for m in range(1, n):
                    acc = acc + expo[i][m] * expo[m][k]
                nxt[i][k] = acc
        expo = nxt
    trace = expo[0][0] + expo[1][1] + expo[2][2] + expo[3][3]
    inv = 1.0 / trace
    wt = [[expo[i][k] * inv for k in range(n)] for i in range(n)]
    soft = zero
    gbias = zero
    for i in range(n):
        for k in range(n):
            if abs(i - k) <= 1:
                soft = soft + wt[i][k] * tri[i][k]
            gbias = gbias + wt[i][k] * (leads[i] * leads[k])

    def scaled_by(val, *which):
        for i in which:
            if i == 0:
                val = val * fac
        return val

    for i in range(n):
        for k in range(n):
            coef[base + i * n + k] = unit_count * scaled_by(wt[i][k], i, k)
    for k in range(n):
        val = wt[0][k] * leads[0]
        for i in range(1, n):
            val = val + wt[i][k] * leads[i]
        coef[base + n * n + k] = math.sqrt(unit_count) * scaled_by(val, k)
    return gbias, soft


def kernel_body(
    sections,
    unit_count,
    labels_hbm,
    lead0_hbm,
    bias_hbm,
    start_hbm,
    diag_hbm,
    coup_hbm,
    table_hbm,
    kern_hbm,
    grad_diag,
    grad_coup,
    grad_lin,
    small,
    last_z,
    last_img,
    last_coef,
    z,
    img,
    rec,
    send_img,
    send_scl,
    w_buf,
    back,
    xh,
    xl,
    wf,
    wb,
    part,
    coef,
    lead_b,
    alpha_b,
    beta_b,
    fac_b,
    pk,
    gath,
    rly,
    diag,
    coup,
    table,
    kern,
    s_img_s,
    s_img_r,
    s_scl_s,
    s_scl_r,
    s_pk_s,
    s_pk_r,
    s_in_s,
    s_in_r,
    s_out_s,
    s_out_r,
    labels,
    lead0,
    bias,
    s_load,
    s_one,
    s_keep,
):
    me = lax.axis_index("layer")
    per, rows, width = z.shape[1:]
    num_groups = width // LANES
    half = LANES // 2
    block_rows = per * rows
    last = ITERS - 1

    barrier = pltpu.get_barrier_semaphore()
    for hop in range(1, sections):
        peer = lax.rem(me + hop, sections)
        pl.semaphore_signal(barrier, inc=1, device_id={"layer": peer}, device_id_type=MESH)

    def load_kern():
        return pltpu.make_async_copy(kern_hbm, kern, s_one.at[0])

    def load_table():
        return pltpu.make_async_copy(table_hbm, table, s_one.at[1])

    def load(which, c):
        src, dst = ((start_hbm, z), (coup_hbm, coup), (diag_hbm, diag))[which]
        return pltpu.make_async_copy(src.at[c], dst.at[c], s_load.at[which, c])

    def load_row(which):
        src, dst = ((lead0_hbm, lead0), (labels_hbm, labels), (bias_hbm, bias))[which]
        return pltpu.make_async_copy(src, dst, s_one.at[2 + which])

    load(0, 0).start()
    load(1, 0).start()
    load_kern().start()
    load_kern().wait()
    chan = kern.shape[-1]
    zero_tap = jnp.zeros((chan, chan), jnp.float32)

    def lay_out(taps, out, tap_row):
        for in_pos in range(4):
            pieces = [taps[in_pos - q] if 0 <= in_pos - q <= 2 else zero_tap for q in range(2)]
            val = jnp.concatenate(pieces, axis=1)
            top = val.astype(jnp.bfloat16)
            at = slice(in_pos * chan, (in_pos + 1) * chan)
            out[at, tap_row * LANES : (tap_row + 1) * LANES] = top
            out[at, (3 + tap_row) * LANES : (4 + tap_row) * LANES] = (val - top.astype(jnp.float32)).astype(jnp.bfloat16)

    for tap_row in range(3):
        lay_out([kern[tap_row, tap] for tap in range(3)], wf, tap_row)

    relayed = sections == RELAY_SECTIONS
    low, high = sections // 2 - 1, sections // 2
    img_via, scl_via = sections - 1, 0
    direct = per // 2
    near = jnp.logical_and

    def relay_in(t, images):
        src = send_img if images else send_scl
        return pltpu.make_async_remote_copy(
            src_ref=src.at[t, pl.ds(direct, per - direct)],
            dst_ref=rly.at[t],
            send_sem=s_in_s.at[t],
            recv_sem=s_in_r.at[t],
            device_id={"layer": jnp.int32(img_via if images else scl_via)},
            device_id_type=MESH,
        )

    def relay_out(t, images):
        dst = img if images else rec
        return pltpu.make_async_remote_copy(
            src_ref=rly.at[t],
            dst_ref=dst.at[t, pl.ds(direct, per - direct)],
            send_sem=s_out_s.at[t],
            recv_sem=s_out_r.at[t],
            device_id={"layer": jnp.int32(high if images else low)},
            device_id_type=MESH,
        )

    def pass_on(t, scaled_too):
        if not relayed:
            return
        for images, via in ((False, scl_via), (True, img_via)):
            if images or scaled_too:

                @pl.when(me == via)
                def _():
                    relay_in(t, images).wait_recv()
                    relay_out(t, images).start()

    def img_copy(t, count=per):
        return pltpu.make_async_remote_copy(
            src_ref=send_img.at[t, pl.ds(0, count)],
            dst_ref=img.at[t, pl.ds(0, count)],
            send_sem=s_img_s.at[t],
            recv_sem=s_img_r.at[t],
            device_id={"layer": lax.rem(me + 1, sections)},
            device_id_type=MESH,
        )

    def scl_copy(t, count=per):
        return pltpu.make_async_remote_copy(
            src_ref=send_scl.at[t, pl.ds(0, count)],
            dst_ref=rec.at[t, pl.ds(0, count)],
            send_sem=s_scl_s.at[t],
            recv_sem=s_scl_r.at[t],
            device_id={"layer": lax.rem(me + sections - 1, sections)},
            device_id_type=MESH,
        )

    def each_copy(t, images, side, act):
        copy = img_copy if images else scl_copy
        if images:
            has = me < sections - 1 if side == 0 else me > 0
            middle = low if side == 0 else high
        else:
            has = me > 0 if side == 0 else me < sections - 1
            middle = high if side == 0 else low
        if not relayed:

            @pl.when(has)
            def _():
                act(copy(t))

            return

        @pl.when(near(has, me != middle))
        def _():
            act(copy(t))

        @pl.when(me == middle)
        def _():
            act(relay_in(t, images) if side == 0 else relay_out(t, images))
            act(copy(t, direct))

    def pk_copy(j, c, hop):
        slot = (j % 2) * CHUNKS + c
        return pltpu.make_async_remote_copy(
            src_ref=pk.at[slot],
            dst_ref=gath.at[slot, me],
            send_sem=s_pk_s.at[slot, hop],
            recv_sem=s_pk_r.at[slot, hop],
            device_id={"layer": lax.rem(me + hop, sections)},
            device_id_type=MESH,
        )

    def start_copy(copy):
        copy.start()

    def await_recv(copy):
        copy.wait_recv()

    def await_send(copy):
        copy.wait_send()

    row_id = lax.broadcasted_iota(jnp.int32, (per, LANES), 0)
    lane_id = lax.broadcasted_iota(jnp.int32, (per, LANES), 1)

    def spread_row(values, c):
        out = jnp.zeros((per, LANES), jnp.float32)
        for s in range(per):
            out = jnp.where(row_id == s, values[c * per + s], out)
        return out

    def put_shifted(s, val):
        wide = jnp.concatenate([val, jnp.zeros((rows, LANES), jnp.float32)], axis=1)
        wide = pltpu.roll(wide, half, 1)
        top = wide.astype(jnp.bfloat16)
        at = pl.ds(pl.multiple_of(s * rows, rows), rows)
        xh[at, :] = top
        xl[at, :] = (wide - top.astype(jnp.float32)).astype(jnp.bfloat16)

    def conv(wts, out_ref, t):
        row = lax.rem(lax.broadcasted_iota(jnp.int32, (block_rows, LANES), 0), rows)
        cols = [slice(g * LANES, (g + 2) * LANES) for g in range(num_groups)]
        a_hi = jnp.concatenate([xh[:, at] for at in cols], axis=0)
        a_lo = jnp.concatenate([xl[:, at] for at in cols], axis=0)
        both = jnp.dot(a_hi, wts[...], preferred_element_type=jnp.float32)
        prod = both[:, : 3 * LANES] + both[:, 3 * LANES :]
        prod += jnp.dot(a_lo, wts[:, : 3 * LANES], preferred_element_type=jnp.float32)
        for g in range(num_groups):
            mine = prod[g * block_rows : (g + 1) * block_rows]
            above = pltpu.roll(mine[:, :LANES], 1, 0)
            below = pltpu.roll(mine[:, 2 * LANES :], block_rows - 1, 0)
            out = mine[:, LANES : 2 * LANES]
            out += jnp.where(row == 0, 0.0, above)
            out += jnp.where(row == rows - 1, 0.0, below)
            out_ref[t, :, :, g * LANES : (g + 1) * LANES] = out.reshape(per, rows, LANES)

    def wide_row(k, s):
        cf = coef[k, pl.ds(s, 1), :]
        return jnp.concatenate([cf] * num_groups, axis=1)

    def fold(val):
        acc = val[:, :LANES]
        for g in range(1, num_groups):
            acc = acc + val[:, g * LANES : (g + 1) * LANES]
        return jnp.sum(acc, axis=0, keepdims=True)

    def forward(t):
        @pl.when(me < sections - 1)
        def _():
            conv(wf, send_img, t)

    def send_images(j, c):
        t = j * CHUNKS + c
        if not relayed or j < last:
            each_copy(t, True, 0, start_copy)
            return

        @pl.when(me != low)
        def _():
            each_copy(t, True, 0, start_copy)

        def late(spot):
            relay_in(spot, True).start()
            img_copy(spot, direct).start()

        @pl.when(near(me == low, c > 0))
        def _():
            late(t - 1)

        @pl.when(near(me == low, c == CHUNKS - 1))
        def _():
            late(t)

    def recur(ref, val, j, t, s):
        val = val * wide_row(1, s) + ref[t - CHUNKS, s] * wide_row(2, s)
        if j > 1:
            val = val + ref[t - 2 * CHUNKS, s] * wide_row(3, s)
        return val

    def totals(j, c, count):
        slot = (j % 2) * CHUNKS + c
        for hop in range(1, sections):
            pk_copy(j, c, hop).wait()
        total = gath[slot, 0]
        for peer in range(1, sections):
            total = total + gath[slot, peer]
        total = jnp.broadcast_to(total, (per, LANES))
        outs = []
        for k in range(count):
            picked = jnp.where(lane_id == k * per + row_id, total, 0.0)
            outs.append(jnp.broadcast_to(jnp.sum(picked, axis=1, keepdims=True), (per, LANES)))
        return outs

    def rates(j, c):
        t = j * CHUNKS + c
        bias_c = spread_row(bias, c)
        sums = totals(j, c, 4 if j == 0 else 3)
        lead_now = lead_b[t]
        image_lead = bias_c * lead_now + 0.5 * sums[0]
        if j == 0:
            factor = 1.0 / jnp.sqrt(lead_now * lead_now + sums[3])
            fac_b[c] = factor
            alpha = factor * factor * (lead_now * image_lead + sums[1])
            lead_now = lead_now * factor
            image_lead = image_lead * factor
            power = factor * factor * sums[2]
            rest_lead = image_lead - alpha * lead_now
            beta = jnp.sqrt(image_lead * image_lead + power - alpha * alpha + 1e-06)
            lead_b[t] = lead_now
            inv = 1.0 / beta
            coef[1] = inv * factor
            coef[2] = -alpha * inv * factor
        else:
            beta_old = beta_b[t - CHUNKS]
            lead_old = lead_b[t - CHUNKS]
            alpha = lead_now * image_lead + sums[1]
            rest_lead = image_lead - alpha * lead_now - beta_old * lead_old
            beta = jnp.sqrt(image_lead * image_lead + sums[2] - alpha * alpha - beta_old * beta_old + 1e-06)
            inv = 1.0 / beta
            coef[1] = inv
            coef[2] = -alpha * inv
            coef[3] = -beta_old * inv * (fac_b[c] if j == 1 else 1.0)
        lead_b[t + CHUNKS] = rest_lead * inv
        alpha_b[t] = alpha
        beta_b[t] = beta

    def apply(j, c):
        t = j * CHUNKS + c
        final_step = j == last
        if not final_step:
            each_copy(t, False, 1, await_recv)

            @pl.when(me < sections - 1)
            def _():
                def shift_one(s, carry):
                    put_shifted(s, rec[t, s])
                    return carry

                lax.fori_loop(0, per, shift_one, 0, unroll=True)
                conv(wb, back, t)

            @pl.when(me == sections - 1)
            def _():
                back[t] = jnp.zeros((per, rows, width), jnp.float32)

        if j > 0:
            rates(j - 1, c)
        else:
            load(2, c).wait()
        coef[0] = lead_b[t]
        def early(s, carry):
            zs = recur(z, w_buf[c, s], j, t, s)
            z[t, s] = zs
            lin = table[labels[c * per + s]]
            part[0, pl.ds(s, 1), :] = fold(lin * zs)
            w = diag[c, s] * zs + lin * (0.5 * wide_row(0, s))
            part[1, pl.ds(s, 1), :] = fold(zs * w)
            return carry

        def closing_one(s, carry):
            image = recur(img, img[t, s], j, t, s)
            img[t, s] = image
            part[1, pl.ds(s, 1), :] -= fold(z[t, s] * (coup[c, s] * image))
            return carry

        if final_step:
            lax.fori_loop(0, per, early, 0, unroll=True)
        each_copy(t, True, 1, await_recv)

        @pl.when(me == 0)
        def _():
            img[t] = jnp.zeros((per, rows, width), jnp.float32)

        def one(s, carry):
            if j > 0:
                zs = recur(z, w_buf[c, s], j, t, s)
                z[t, s] = zs
                image = recur(img, img[t, s], j, t, s)
                img[t, s] = image
            else:
                zs = z[t, s]
                image = img[t, s]
            lin = table[labels[c * per + s]]
            pulled = back[t, s]
            if j > 0:
                pulled = recur(back, pulled, j, t, s)
                if j + 1 < last:
                    back[t, s] = pulled
            w = diag[c, s] * zs - 0.5 * (coup[c, s] * image + pulled)
            w = w + lin * (0.5 * wide_row(0, s))
            part[0, pl.ds(s, 1), :] = fold(lin * zs)
            part[1, pl.ds(s, 1), :] = fold(zs * w)
            w_buf[c, s] = w
            put_shifted(s, w)
            if j + 1 < last:
                send_scl[t + CHUNKS, s] = coup[c, s] * w
            part[2, pl.ds(s, 1), :] = fold(w * w)
            if j == 0:
                part[3, pl.ds(s, 1), :] = fold(zs * zs)
            return carry

        lax.fori_loop(0, per, closing_one if final_step else one, 0, unroll=2)
        if j + 1 < last:
            each_copy(t + CHUNKS, False, 0, start_copy)
        packet = jnp.zeros((per, LANES), jnp.float32)
        for k in range(4 if j == 0 else (2 if final_step else 3)):
            packet = jnp.where(lane_id == k * per + row_id, jnp.sum(part[k], axis=1, keepdims=True), packet)
        packet = jnp.sum(packet, axis=0, keepdims=True)
        slot = (j % 2) * CHUNKS + c
        pk[slot] = packet
        gath[slot, me] = packet
        for hop in range(1, sections):
            pk_copy(j, c, hop).start()

    def finish(c, with_grads):
        t = last * CHUNKS + c
        bias_c = spread_row(bias, c)
        sums = totals(last, c, 2)
        lead_now = lead_b[t]
        alpha = lead_now * (bias_c * lead_now + 0.5 * sums[0]) + sums[1]
        alphas = [alpha_b[j * CHUNKS + c] for j in range(last)] + [alpha]
        betas = [beta_b[j * CHUNKS + c] for j in range(last)]
        leads = [lead_b[j * CHUNKS + c] for j in range(ITERS)]
        if not with_grads:
            for k, val in enumerate(alphas + betas + leads + [fac_b[c]]):
                last_coef[k] = val
            return

        gbias, soft = mixing(alphas, betas, leads, fac_b[c], unit_count, coef, 4)
        mine = lane_id == c * per + row_id
        for k, val in enumerate((gbias, soft)):
            small[k : k + 1, :] += jnp.sum(jnp.where(mine, val, 0.0), axis=0, keepdims=True)
        n = ITERS

        def final(s, carry):
            cf = [coef[4 + k, pl.ds(s, 1), :] for k in range(n * n + n)]

            def parts(cols):
                return [[ref[i * CHUNKS + c, s, :, cols] for i in range(n)] for ref in (z, img)]

            def put(cols, values):
                for ref, val in zip((grad_diag, grad_coup, grad_lin), values):
                    ref[c, s, :, cols] = val

            gradients(cf, num_groups, parts, put)
            return carry

        lax.fori_loop(0, per, final, 0, unroll=2)

    def begin(c, carry):
        load(0, c).wait()
        load(1, c).wait()

        @pl.when(c == 0)
        def _():
            for other in range(1, CHUNKS):
                load(0, other).start()
                load(1, other).start()
            for which in range(3):
                load_row(which).start()
            load_table().start()
            for other in range(CHUNKS):
                load(2, other).start()

        def first(s, carry):
            val = z[c, s]
            send_scl[c, s] = coup[c, s] * val
            put_shifted(s, val)
            return carry

        lax.fori_loop(0, per, first, 0, unroll=True)

        @pl.when(me < sections - 1)
        def _():
            conv(wf, send_img, c)

        @pl.when(c == 0)
        def _():
            pl.semaphore_wait(barrier, sections - 1)

        each_copy(c, False, 0, start_copy)
        each_copy(c, True, 0, start_copy)
        return carry

    small[...] = jnp.zeros((2, LANES), jnp.float32)
    lax.fori_loop(0, CHUNKS, begin, 0)
    for tap_row in range(3):
        lay_out([jnp.transpose(kern[2 - tap_row, 2 - tap]) for tap in range(3)], wb, tap_row)
    load_table().wait()
    for which in range(3):
        load_row(which).wait()

    def spread_lead(c, carry):
        lead_b[c] = spread_row(lead0, c)
        return carry

    lax.fori_loop(0, CHUNKS, spread_lead, 0)

    def pass_first(c, carry):
        pass_on(c, True)
        return carry

    lax.fori_loop(0, CHUNKS, pass_first, 0)

    for j in range(last):

        def step(c, carry):
            ahead = 1 if j + 1 < last else 2

            @pl.when(c >= ahead)
            def _():
                pass_on((j + 1) * CHUNKS + c - ahead, j + 1 < last)

            if j > 0:

                @pl.when(c == 0)
                def _():
                    pass_on((j + 1) * CHUNKS - 1, True)

            apply(j, c)
            forward((j + 1) * CHUNKS + c)
            send_images(j + 1, c)
            return carry

        lax.fori_loop(0, CHUNKS, step, 0)

    pass_on(ITERS * CHUNKS - 2, False)
    pass_on(ITERS * CHUNKS - 1, False)

    def settle(t, carry):
        each_copy(t, True, 0, await_send)
        if relayed:

            @pl.when(me == img_via)
            def _():
                relay_out(t, True).wait_send()

        return carry

    def settle_scaled(t, carry):
        each_copy(t, False, 0, await_send)
        if relayed:

            @pl.when(me == scl_via)
            def _():
                relay_out(t, False).wait_send()

        return carry

    def closing(c, carry):
        for j in range(last):
            settle(j * CHUNKS + c, 0)
            settle_scaled(j * CHUNKS + c, 0)
        apply(last, c)
        return carry

    def ending(c, carry):
        finish(c, True)
        return carry

    lax.fori_loop(0, CHUNKS, closing, 0)
    lax.fori_loop(last * CHUNKS, ITERS * CHUNKS, settle, 0)
    keeps = [
        pltpu.make_async_copy(src.at[j * CHUNKS + CHUNKS - 1], dst.at[j], s_keep.at[which, j])
        for which, (src, dst) in enumerate(((z, last_z), (img, last_img)))
        for j in range(ITERS)
    ]
    for keep in keeps:
        keep.start()
    lax.fori_loop(0, CHUNKS - 1, ending, 0)
    for keep in keeps:
        keep.wait()
    finish(CHUNKS - 1, False)


def hand_over(unit_count, in_d, in_c, in_l, small, zs, ims, known, out_d, out_c, out_l, gbias, soft, sums, row_b, row_s, new, coef, sems):
    pairs = ((in_d, out_d), (in_c, out_c), (in_l, out_l))
    old = pl.ds(0, CHUNKS - 1)
    fetch = pltpu.make_async_copy(small, sums, sems.at[8])
    fetch.start()
    moves = [pltpu.make_async_copy(src.at[old], dst.at[old], sems.at[which]) for which, (src, dst) in enumerate(pairs)]
    for move in moves:
        move.start()
    count = coef.shape[0]
    per, width = zs.shape[1], zs.shape[-1]
    n = ITERS
    rows_in = [known[k] for k in range(3 * n)]
    bias_part, soft_part = mixing(rows_in[:n], rows_in[n : 2 * n - 1], rows_in[2 * n - 1 : 3 * n - 1], rows_in[3 * n - 1], unit_count, coef, 0)

    def final(s, carry):
        cf = [coef[k, pl.ds(s, 1), :] for k in range(count)]

        def parts(cols):
            return [[ref[i, s, :, cols] for i in range(ITERS)] for ref in (zs, ims)]

        def put(cols, values):
            for which, val in enumerate(values):
                new[which, s, :, cols] = val

        gradients(cf, width // LANES, parts, put)
        return carry

    lax.fori_loop(0, per, final, 0, unroll=2)
    moves += [pltpu.make_async_copy(new.at[which], dst.at[CHUNKS - 1], sems.at[3 + which]) for which, (_, dst) in enumerate(pairs)]
    for move in moves[3:]:
        move.start()
    fetch.wait()
    specs = gbias.shape[0]
    lane = lax.broadcasted_iota(jnp.int32, (per, LANES), 1)
    mine = lane == (CHUNKS - 1) * per + lax.broadcasted_iota(jnp.int32, (per, LANES), 0)
    for k, (row, part) in enumerate(((row_b, bias_part), (row_s, soft_part))):
        whole = sums[k : k + 1, :] + jnp.sum(jnp.where(mine, part, 0.0), axis=0, keepdims=True)
        row[...] = whole[0, :specs]
    rows = [pltpu.make_async_copy(row_b, gbias, sems.at[6]), pltpu.make_async_copy(row_s, soft, sems.at[7])]
    for row in rows:
        row.start()
    for move in moves + rows:
        move.wait()


def in_hbm(array):
    return pltpu.with_memory_space_constraint(array, pltpu.HBM)


def body(start_lead, start_field, diag_dual, coupling_dual, linear_table, labels, bias_dual, kernels):
    sections = lax.axis_size("layer")
    specs, _, rows, width = start_field.shape
    unit_count = sections * rows * width
    per = specs // CHUNKS
    chan = kernels.shape[-1]
    block = (per, rows, width)
    shape = (CHUNKS,) + block
    full = pl.BlockSpec(memory_space=pltpu.VMEM)
    anywhere = pl.BlockSpec(memory_space=pl.ANY)
    f32, bf16 = jnp.float32, jnp.bfloat16
    dma = pltpu.SemaphoreType.DMA
    slots, sent = ITERS * CHUNKS, (ITERS - 1) * CHUNKS
    small_block = (per, LANES)
    outs = pl.pallas_call(
        functools.partial(kernel_body, sections, float(unit_count)),
        out_shape=[pltpu.VMEM(shape, f32)] * 3 + [pltpu.VMEM((2, LANES), f32)] + [pltpu.VMEM((ITERS,) + block, f32)] * 2 + [pltpu.VMEM((3 * ITERS,) + small_block, f32)],
        in_specs=[anywhere] * 8,
        out_specs=[full] * 7,
        scratch_shapes=[
            pltpu.VMEM((slots,) + block, f32),
            pltpu.VMEM((slots,) + block, f32),
            pltpu.VMEM((sent,) + block, f32),
            pltpu.VMEM((slots,) + block, f32),
            pltpu.VMEM((sent,) + block, f32),
            pltpu.VMEM(shape, f32),
            pltpu.VMEM((sent,) + block, f32),
            pltpu.VMEM((per * rows, width + LANES), bf16),
            pltpu.VMEM((per * rows, width + LANES), bf16),
            pltpu.VMEM((4 * chan, 12 * chan), bf16),
            pltpu.VMEM((4 * chan, 12 * chan), bf16),
            pltpu.VMEM((4,) + small_block, f32),
            pltpu.VMEM((24,) + small_block, f32),
            pltpu.VMEM((slots,) + small_block, f32),
            pltpu.VMEM((slots,) + small_block, f32),
            pltpu.VMEM((slots,) + small_block, f32),
            pltpu.VMEM((CHUNKS,) + small_block, f32),
            pltpu.VMEM((2 * CHUNKS, 1, LANES), f32),
            pltpu.VMEM((2 * CHUNKS, sections, 1, LANES), f32),
            pltpu.VMEM((slots, per - per // 2, rows, width), f32),
            pltpu.VMEM(shape, f32),
            pltpu.VMEM(shape, f32),
            pltpu.VMEM((linear_table.shape[0], rows, width), f32),
            pltpu.VMEM(kernels.shape[1:], f32),
            dma((slots,)),
            dma((slots,)),
            dma((sent,)),
            dma((sent,)),
            dma((2 * CHUNKS, sections)),
            dma((2 * CHUNKS, sections)),
            dma((slots,)),
            dma((slots,)),
            dma((slots,)),
            dma((slots,)),
            pltpu.SMEM((specs,), jnp.int32),
            pltpu.SMEM((specs,), f32),
            pltpu.SMEM((specs,), f32),
            dma((3, CHUNKS)),
            dma((5,)),
            dma((2, ITERS)),
        ],
        compiler_params=pltpu.CompilerParams(collective_id=0, has_side_effects=True, vmem_limit_bytes=44 * 1024 * 1024),
    )(
        in_hbm(labels),
        in_hbm(start_lead),
        in_hbm(bias_dual),
        in_hbm(start_field.reshape(shape)),
        in_hbm(diag_dual.reshape(shape)),
        in_hbm(coupling_dual.reshape(shape)),
        in_hbm(linear_table.reshape(linear_table.shape[0], rows, width)),
        in_hbm(kernels.reshape(kernels.shape[1:])),
    )
    done = pl.pallas_call(
        functools.partial(hand_over, float(unit_count)),
        out_shape=[jax.ShapeDtypeStruct(shape, f32)] * 3 + [jax.ShapeDtypeStruct((specs,), f32)] * 2,
        in_specs=[anywhere] * 4 + [full] * 3,
        out_specs=[anywhere] * 5,
        scratch_shapes=[pltpu.VMEM((2, LANES), f32), pltpu.VMEM((specs,), f32), pltpu.VMEM((specs,), f32), pltpu.VMEM((3,) + block, f32), pltpu.VMEM((20,) + small_block, f32), dma((9,))],
        compiler_params=pltpu.CompilerParams(vmem_limit_bytes=8 * 1024 * 1024),
    )(*outs)
    big = [out.reshape(start_field.shape) for out in done[:3]]
    return (*big, done[3], done[4])


def solution(mesh):
    placed = (
        P("spec"),
        P("spec", "layer", None, None),
        P("spec", "layer", None, None),
        P("spec", "layer", None, None),
        P(None, "layer", None, None),
        P("spec"),
        P("spec"),
        P("layer", None, None, None, None),
    )
    return jax.shard_map(
        body,
        mesh=mesh,
        in_specs=placed,
        out_specs=(
            P("spec", "layer", None, None),
            P("spec", "layer", None, None),
            P("spec", "layer", None, None),
            P("spec"),
            P("spec"),
        ),
        check_vma=False,
    )
```

```python
import functools
import math

import jax
import jax.numpy as jnp
from jax import lax
from jax.experimental import pallas as pl
from jax.experimental.pallas import tpu as pltpu
from jax.sharding import PartitionSpec as P

ITERS = 4
CHUNKS = 4
LANES = 128
RELAY_SECTIONS = 8
MESH = pl.DeviceIdType.MESH


def gradients(cf, num_groups, parts, put):
    n = ITERS
    for g in range(num_groups):
        cols = slice(g * LANES, (g + 1) * LANES)
        zs, ims = parts(cols)
        gd = gc = gl = None
        for k in range(n):
            mixed = zs[0] * cf[k]
            for i in range(1, n):
                mixed = mixed + zs[i] * cf[i * n + k]
            lin = zs[k] * cf[n * n + k]
            if k == 0:
                gd, gc, gl = zs[k] * mixed, -(ims[k] * mixed), lin
            else:
                gd, gc, gl = gd + zs[k] * mixed, gc - ims[k] * mixed, gl + lin
        put(cols, (gd, gc, gl))


def mixing(alphas, betas, leads, fac, unit_count, coef, base):
    n = ITERS
    zero = jnp.zeros_like(alphas[0])
    tri = [[zero] * n for _ in range(n)]
    norm = zero
    for i in range(n):
        tri[i][i] = alphas[i]
        norm = norm + alphas[i] * alphas[i]
        if i + 1 < n:
            tri[i][i + 1] = betas[i]
            tri[i + 1][i] = betas[i]
            norm = norm + 2.0 * (betas[i] * betas[i])
    scale = 0.5 / jnp.sqrt(norm)
    sx = [[tri[i][k] * scale for k in range(n)] for i in range(n)]
    expo = [[zero + (1.0 if i == k else 0.0) for k in range(n)] for i in range(n)]
    for degree in range(12, 0, -1):
        nxt = []
        for i in range(n):
            line = []
            for k in range(n):
                acc = None
                for m in range(max(0, i - 1), min(n, i + 2)):
                    term = sx[i][m] * expo[m][k]
                    acc = term if acc is None else acc + term
                acc = acc * (1.0 / degree)
                line.append(acc + 1.0 if i == k else acc)
            nxt.append(line)
        expo = nxt
    for _ in range(4):
        nxt = [[None] * n for _ in range(n)]
        for i in range(n):
            for k in range(n):
                acc = expo[i][0] * expo[0][k]
                for m in range(1, n):
                    acc = acc + expo[i][m] * expo[m][k]
                nxt[i][k] = acc
        expo = nxt
    trace = expo[0][0] + expo[1][1] + expo[2][2] + expo[3][3]
    inv = 1.0 / trace
    wt = [[expo[i][k] * inv for k in range(n)] for i in range(n)]
    soft = zero
    gbias = zero
    for i in range(n):
        for k in range(n):
            if abs(i - k) <= 1:
                soft = soft + wt[i][k] * tri[i][k]
            gbias = gbias + wt[i][k] * (leads[i] * leads[k])

    def scaled_by(val, *which):
        for i in which:
            if i == 0:
                val = val * fac
        return val

    for i in range(n):
        for k in range(n):
            coef[base + i * n + k] = unit_count * scaled_by(wt[i][k], i, k)
    for k in range(n):
        val = wt[0][k] * leads[0]
        for i in range(1, n):
            val = val + wt[i][k] * leads[i]
        coef[base + n * n + k] = math.sqrt(unit_count) * scaled_by(val, k)
    return gbias, soft


def kernel_body(
    sections,
    unit_count,
    labels_hbm,
    lead0_hbm,
    bias_hbm,
    start_hbm,
    diag_hbm,
    coup_hbm,
    table_hbm,
    kern_hbm,
    grad_diag,
    grad_coup,
    grad_lin,
    small,
    last_z,
    last_img,
    last_coef,
    z,
    img,
    rec,
    send_img,
    send_scl,
    w_buf,
    back,
    xh,
    xl,
    wf,
    wb,
    part,
    coef,
    lead_b,
    alpha_b,
    beta_b,
    fac_b,
    pk,
    gath,
    rly,
    diag,
    coup,
    table,
    kern,
    s_img_s,
    s_img_r,
    s_scl_s,
    s_scl_r,
    s_pk_s,
    s_pk_r,
    s_in_s,
    s_in_r,
    s_out_s,
    s_out_r,
    labels,
    lead0,
    bias,
    s_load,
    s_one,
    s_keep,
):
    me = lax.axis_index("layer")
    per, rows, width = z.shape[1:]
    num_groups = width // LANES
    half = LANES // 2
    block_rows = per * rows
    last = ITERS - 1

    barrier = pltpu.get_barrier_semaphore()
    for hop in range(1, sections):
        peer = lax.rem(me + hop, sections)
        pl.semaphore_signal(barrier, inc=1, device_id={"layer": peer}, device_id_type=MESH)

    def load_kern():
        return pltpu.make_async_copy(kern_hbm, kern, s_one.at[0])

    def load_table():
        return pltpu.make_async_copy(table_hbm, table, s_one.at[1])

    def load(which, c):
        src, dst = ((start_hbm, z), (coup_hbm, coup), (diag_hbm, diag))[which]
        return pltpu.make_async_copy(src.at[c], dst.at[c], s_load.at[which, c])

    def load_row(which):
        src, dst = ((lead0_hbm, lead0), (labels_hbm, labels), (bias_hbm, bias))[which]
        return pltpu.make_async_copy(src, dst, s_one.at[2 + which])

    load(0, 0).start()
    load(1, 0).start()
    load_kern().start()
    load_kern().wait()
    chan = kern.shape[-1]
    zero_tap = jnp.zeros((chan, chan), jnp.float32)

    def lay_out(taps, out, tap_row):
        for in_pos in range(4):
            pieces = [taps[in_pos - q] if 0 <= in_pos - q <= 2 else zero_tap for q in range(2)]
            val = jnp.concatenate(pieces, axis=1)
            top = val.astype(jnp.bfloat16)
            at = slice(in_pos * chan, (in_pos + 1) * chan)
            out[at, tap_row * LANES : (tap_row + 1) * LANES] = top
            out[at, (3 + tap_row) * LANES : (4 + tap_row) * LANES] = (val - top.astype(jnp.float32)).astype(jnp.bfloat16)

    for tap_row in range(3):
        lay_out([kern[tap_row, tap] for tap in range(3)], wf, tap_row)

    relayed = sections == RELAY_SECTIONS
    low, high = sections // 2 - 1, sections // 2
    img_via, scl_via = sections - 1, 0
    direct = per // 2
    near = jnp.logical_and

    def relay_in(t, images):
        src = send_img if images else send_scl
        return pltpu.make_async_remote_copy(
            src_ref=src.at[t, pl.ds(direct, per - direct)],
            dst_ref=rly.at[t],
            send_sem=s_in_s.at[t],
            recv_sem=s_in_r.at[t],
            device_id={"layer": jnp.int32(img_via if images else scl_via)},
            device_id_type=MESH,
        )

    def relay_out(t, images):
        dst = img if images else rec
        return pltpu.make_async_remote_copy(
            src_ref=rly.at[t],
            dst_ref=dst.at[t, pl.ds(direct, per - direct)],
            send_sem=s_out_s.at[t],
            recv_sem=s_out_r.at[t],
            device_id={"layer": jnp.int32(high if images else low)},
            device_id_type=MESH,
        )

    def pass_on(t, scaled_too):
        if not relayed:
            return
        for images, via in ((False, scl_via), (True, img_via)):
            if images or scaled_too:

                @pl.when(me == via)
                def _():
                    relay_in(t, images).wait_recv()
                    relay_out(t, images).start()

    def img_copy(t, count=per):
        return pltpu.make_async_remote_copy(
            src_ref=send_img.at[t, pl.ds(0, count)],
            dst_ref=img.at[t, pl.ds(0, count)],
            send_sem=s_img_s.at[t],
            recv_sem=s_img_r.at[t],
            device_id={"layer": lax.rem(me + 1, sections)},
            device_id_type=MESH,
        )

    def scl_copy(t, count=per):
        return pltpu.make_async_remote_copy(
            src_ref=send_scl.at[t, pl.ds(0, count)],
            dst_ref=rec.at[t, pl.ds(0, count)],
            send_sem=s_scl_s.at[t],
            recv_sem=s_scl_r.at[t],
            device_id={"layer": lax.rem(me + sections - 1, sections)},
            device_id_type=MESH,
        )

    def each_copy(t, images, side, act):
        copy = img_copy if images else scl_copy
        if images:
            has = me < sections - 1 if side == 0 else me > 0
            middle = low if side == 0 else high
        else:
            has = me > 0 if side == 0 else me < sections - 1
            middle = high if side == 0 else low
        if not relayed:

            @pl.when(has)
            def _():
                act(copy(t))

            return

        @pl.when(near(has, me != middle))
        def _():
            act(copy(t))

        @pl.when(me == middle)
        def _():
            act(relay_in(t, images) if side == 0 else relay_out(t, images))
            act(copy(t, direct))

    def pk_copy(j, c, hop):
        slot = (j % 2) * CHUNKS + c
        return pltpu.make_async_remote_copy(
            src_ref=pk.at[slot],
            dst_ref=gath.at[slot, me],
            send_sem=s_pk_s.at[slot, hop],
            recv_sem=s_pk_r.at[slot, hop],
            device_id={"layer": lax.rem(me + hop, sections)},
            device_id_type=MESH,
        )

    def start_copy(copy):
        copy.start()

    def await_recv(copy):
        copy.wait_recv()

    def await_send(copy):
        copy.wait_send()

    row_id = lax.broadcasted_iota(jnp.int32, (per, LANES), 0)
    lane_id = lax.broadcasted_iota(jnp.int32, (per, LANES), 1)

    def spread_row(values, c):
        out = jnp.zeros((per, LANES), jnp.float32)
        for s in range(per):
            out = jnp.where(row_id == s, values[c * per + s], out)
        return out

    def put_shifted(s, val):
        wide = jnp.concatenate([val, jnp.zeros((rows, LANES), jnp.float32)], axis=1)
        wide = pltpu.roll(wide, half, 1)
        top = wide.astype(jnp.bfloat16)
        at = pl.ds(pl.multiple_of(s * rows, rows), rows)
        xh[at, :] = top
        xl[at, :] = (wide - top.astype(jnp.float32)).astype(jnp.bfloat16)

    def conv(wts, out_ref, t):
        row = lax.rem(lax.broadcasted_iota(jnp.int32, (block_rows, LANES), 0), rows)
        cols = [slice(g * LANES, (g + 2) * LANES) for g in range(num_groups)]
        a_hi = jnp.concatenate([xh[:, at] for at in cols], axis=0)
        a_lo = jnp.concatenate([xl[:, at] for at in cols], axis=0)
        both = jnp.dot(a_hi, wts[...], preferred_element_type=jnp.float32)
        prod = both[:, : 3 * LANES] + both[:, 3 * LANES :]
        prod += jnp.dot(a_lo, wts[:, : 3 * LANES], preferred_element_type=jnp.float32)
        for g in range(num_groups):
            mine = prod[g * block_rows : (g + 1) * block_rows]
            above = pltpu.roll(mine[:, :LANES], 1, 0)
            below = pltpu.roll(mine[:, 2 * LANES :], block_rows - 1, 0)
            out = mine[:, LANES : 2 * LANES]
            out += jnp.where(row == 0, 0.0, above)
            out += jnp.where(row == rows - 1, 0.0, below)
            out_ref[t, :, :, g * LANES : (g + 1) * LANES] = out.reshape(per, rows, LANES)

    def wide_row(k, s):
        cf = coef[k, pl.ds(s, 1), :]
        return jnp.concatenate([cf] * num_groups, axis=1)

    def fold(val):
        acc = val[:, :LANES]
        for g in range(1, num_groups):
            acc = acc + val[:, g * LANES : (g + 1) * LANES]
        return jnp.sum(acc, axis=0, keepdims=True)

    def forward(t):
        @pl.when(me < sections - 1)
        def _():
            conv(wf, send_img, t)

    def send_images(j, c):
        t = j * CHUNKS + c
        if not relayed or j < last:
            each_copy(t, True, 0, start_copy)
            return

        @pl.when(me != low)
        def _():
            each_copy(t, True, 0, start_copy)

        def late(spot):
            relay_in(spot, True).start()
            img_copy(spot, direct).start()

        @pl.when(near(me == low, c > 0))
        def _():
            late(t - 1)

        @pl.when(near(me == low, c == CHUNKS - 1))
        def _():
            late(t)

    def recur(ref, val, j, t, s):
        val = val * wide_row(1, s) + ref[t - CHUNKS, s] * wide_row(2, s)
        if j > 1:
            val = val + ref[t - 2 * CHUNKS, s] * wide_row(3, s)
        return val

    def totals(j, c, count):
        slot = (j % 2) * CHUNKS + c
        for hop in range(1, sections):
            pk_copy(j, c, hop).wait()
        total = gath[slot, 0]
        for peer in range(1, sections):
            total = total + gath[slot, peer]
        total = jnp.broadcast_to(total, (per, LANES))
        outs = []
        for k in range(count):
            picked = jnp.where(lane_id == k * per + row_id, total, 0.0)
            outs.append(jnp.broadcast_to(jnp.sum(picked, axis=1, keepdims=True), (per, LANES)))
        return outs

    def rates(j, c):
        t = j * CHUNKS + c
        bias_c = spread_row(bias, c)
        sums = totals(j, c, 4 if j == 0 else 3)
        lead_now = lead_b[t]
        image_lead = bias_c * lead_now + 0.5 * sums[0]
        if j == 0:
            factor = 1.0 / jnp.sqrt(lead_now * lead_now + sums[3])
            fac_b[c] = factor
            alpha = factor * factor * (lead_now * image_lead + sums[1])
            lead_now = lead_now * factor
            image_lead = image_lead * factor
            power = factor * factor * sums[2]
            rest_lead = image_lead - alpha * lead_now
            beta = jnp.sqrt(image_lead * image_lead + power - alpha * alpha + 1e-06)
            lead_b[t] = lead_now
            inv = 1.0 / beta
            coef[1] = inv * factor
            coef[2] = -alpha * inv * factor
        else:
            beta_old = beta_b[t - CHUNKS]
            lead_old = lead_b[t - CHUNKS]
            alpha = lead_now * image_lead + sums[1]
            rest_lead = image_lead - alpha * lead_now - beta_old * lead_old
            beta = jnp.sqrt(image_lead * image_lead + sums[2] - alpha * alpha - beta_old * beta_old + 1e-06)
            inv = 1.0 / beta
            coef[1] = inv
            coef[2] = -alpha * inv
            coef[3] = -beta_old * inv * (fac_b[c] if j == 1 else 1.0)
        lead_b[t + CHUNKS] = rest_lead * inv
        alpha_b[t] = alpha
        beta_b[t] = beta

    def apply(j, c):
        t = j * CHUNKS + c
        final_step = j == last
        if not final_step:
            each_copy(t, False, 1, await_recv)

            @pl.when(me < sections - 1)
            def _():
                def shift_one(s, carry):
                    put_shifted(s, rec[t, s])
                    return carry

                lax.fori_loop(0, per, shift_one, 0, unroll=True)
                conv(wb, back, t)

            @pl.when(me == sections - 1)
            def _():
                back[t] = jnp.zeros((per, rows, width), jnp.float32)

        if j > 0:
            rates(j - 1, c)
        else:
            load(2, c).wait()
        coef[0] = lead_b[t]
        def early(s, carry):
            zs = recur(z, w_buf[c, s], j, t, s)
            z[t, s] = zs
            lin = table[labels[c * per + s]]
            part[0, pl.ds(s, 1), :] = fold(lin * zs)
            w = diag[c, s] * zs + lin * (0.5 * wide_row(0, s))
            part[1, pl.ds(s, 1), :] = fold(zs * w)
            return carry

        def closing_one(s, carry):
            image = recur(img, img[t, s], j, t, s)
            img[t, s] = image
            part[1, pl.ds(s, 1), :] -= fold(z[t, s] * (coup[c, s] * image))
            return carry

        if final_step:
            lax.fori_loop(0, per, early, 0, unroll=True)
        each_copy(t, True, 1, await_recv)

        @pl.when(me == 0)
        def _():
            img[t] = jnp.zeros((per, rows, width), jnp.float32)

        def one(s, carry):
            if j > 0:
                zs = recur(z, w_buf[c, s], j, t, s)
                z[t, s] = zs
                image = recur(img, img[t, s], j, t, s)
                img[t, s] = image
            else:
                zs = z[t, s]
                image = img[t, s]
            lin = table[labels[c * per + s]]
            pulled = back[t, s]
            if j > 0:
                pulled = recur(back, pulled, j, t, s)
                if j + 1 < last:
                    back[t, s] = pulled
            w = diag[c, s] * zs - 0.5 * (coup[c, s] * image + pulled)
            w = w + lin * (0.5 * wide_row(0, s))
            part[0, pl.ds(s, 1), :] = fold(lin * zs)
            part[1, pl.ds(s, 1), :] = fold(zs * w)
            w_buf[c, s] = w
            put_shifted(s, w)
            if j + 1 < last:
                send_scl[t + CHUNKS, s] = coup[c, s] * w
            part[2, pl.ds(s, 1), :] = fold(w * w)
            if j == 0:
                part[3, pl.ds(s, 1), :] = fold(zs * zs)
            return carry

        lax.fori_loop(0, per, closing_one if final_step else one, 0, unroll=2)
        packet = jnp.zeros((per, LANES), jnp.float32)
        for k in range(4 if j == 0 else (2 if final_step else 3)):
            packet = jnp.where(lane_id == k * per + row_id, jnp.sum(part[k], axis=1, keepdims=True), packet)
        packet = jnp.sum(packet, axis=0, keepdims=True)
        slot = (j % 2) * CHUNKS + c
        pk[slot] = packet
        gath[slot, me] = packet
        for hop in range(1, sections):
            pk_copy(j, c, hop).start()
        if j + 1 < last:
            each_copy(t + CHUNKS, False, 0, start_copy)

    def finish(c, with_grads):
        t = last * CHUNKS + c
        bias_c = spread_row(bias, c)
        sums = totals(last, c, 2)
        lead_now = lead_b[t]
        alpha = lead_now * (bias_c * lead_now + 0.5 * sums[0]) + sums[1]
        alphas = [alpha_b[j * CHUNKS + c] for j in range(last)] + [alpha]
        betas = [beta_b[j * CHUNKS + c] for j in range(last)]
        leads = [lead_b[j * CHUNKS + c] for j in range(ITERS)]
        if not with_grads:
            for k, val in enumerate(alphas + betas + leads + [fac_b[c]]):
                last_coef[k] = val
            return

        gbias, soft = mixing(alphas, betas, leads, fac_b[c], unit_count, coef, 4)
        mine = lane_id == c * per + row_id
        for k, val in enumerate((gbias, soft)):
            small[k : k + 1, :] += jnp.sum(jnp.where(mine, val, 0.0), axis=0, keepdims=True)
        n = ITERS

        def final(s, carry):
            cf = [coef[4 + k, pl.ds(s, 1), :] for k in range(n * n + n)]

            def parts(cols):
                return [[ref[i * CHUNKS + c, s, :, cols] for i in range(n)] for ref in (z, img)]

            def put(cols, values):
                for ref, val in zip((grad_diag, grad_coup, grad_lin), values):
                    ref[c, s, :, cols] = val

            gradients(cf, num_groups, parts, put)
            return carry

        lax.fori_loop(0, per, final, 0, unroll=2)

    def begin(c, carry):
        load(0, c).wait()
        load(1, c).wait()

        @pl.when(c == 0)
        def _():
            for other in range(1, CHUNKS):
                load(0, other).start()
                load(1, other).start()
            for which in range(3):
                load_row(which).start()
            load_table().start()
            for other in range(CHUNKS):
                load(2, other).start()

        def first(s, carry):
            val = z[c, s]
            send_scl[c, s] = coup[c, s] * val
            put_shifted(s, val)
            return carry

        lax.fori_loop(0, per, first, 0, unroll=True)

        @pl.when(me < sections - 1)
        def _():
            conv(wf, send_img, c)

        @pl.when(c == 0)
        def _():
            pl.semaphore_wait(barrier, sections - 1)

        each_copy(c, False, 0, start_copy)
        each_copy(c, True, 0, start_copy)
        return carry

    small[...] = jnp.zeros((2, LANES), jnp.float32)
    lax.fori_loop(0, CHUNKS, begin, 0)
    for tap_row in range(3):
        lay_out([jnp.transpose(kern[2 - tap_row, 2 - tap]) for tap in range(3)], wb, tap_row)
    load_table().wait()
    for which in range(3):
        load_row(which).wait()

    def spread_lead(c, carry):
        lead_b[c] = spread_row(lead0, c)
        return carry

    lax.fori_loop(0, CHUNKS, spread_lead, 0)

    def pass_first(c, carry):
        pass_on(c, True)
        return carry

    lax.fori_loop(0, CHUNKS, pass_first, 0)

    for j in range(last):

        def step(c, carry):
            ahead = 1 if j + 1 < last else 2

            @pl.when(c >= ahead)
            def _():
                pass_on((j + 1) * CHUNKS + c - ahead, j + 1 < last)

            if j > 0:

                @pl.when(c == 0)
                def _():
                    pass_on((j + 1) * CHUNKS - 1, True)

            apply(j, c)
            forward((j + 1) * CHUNKS + c)
            send_images(j + 1, c)
            return carry

        lax.fori_loop(0, CHUNKS, step, 0)

    pass_on(ITERS * CHUNKS - 2, False)
    pass_on(ITERS * CHUNKS - 1, False)

    def settle(t, carry):
        each_copy(t, True, 0, await_send)
        if relayed:

            @pl.when(me == img_via)
            def _():
                relay_out(t, True).wait_send()

        return carry

    def settle_scaled(t, carry):
        each_copy(t, False, 0, await_send)
        if relayed:

            @pl.when(me == scl_via)
            def _():
                relay_out(t, False).wait_send()

        return carry

    def closing(c, carry):
        for j in range(last):
            settle(j * CHUNKS + c, 0)
            settle_scaled(j * CHUNKS + c, 0)
        apply(last, c)
        return carry

    def ending(c, carry):
        finish(c, True)
        return carry

    lax.fori_loop(0, CHUNKS, closing, 0)
    lax.fori_loop(last * CHUNKS, ITERS * CHUNKS, settle, 0)
    keeps = [
        pltpu.make_async_copy(src.at[j * CHUNKS + CHUNKS - 1], dst.at[j], s_keep.at[which, j])
        for which, (src, dst) in enumerate(((z, last_z), (img, last_img)))
        for j in range(ITERS)
    ]
    for keep in keeps:
        keep.start()
    lax.fori_loop(0, CHUNKS - 1, ending, 0)
    for keep in keeps:
        keep.wait()
    finish(CHUNKS - 1, False)


def hand_over(unit_count, in_d, in_c, in_l, small, zs, ims, known, out_d, out_c, out_l, gbias, soft, sums, row_b, row_s, new, coef, sems):
    pairs = ((in_d, out_d), (in_c, out_c), (in_l, out_l))
    old = pl.ds(0, CHUNKS - 1)
    fetch = pltpu.make_async_copy(small, sums, sems.at[8])
    fetch.start()
    moves = [pltpu.make_async_copy(src.at[old], dst.at[old], sems.at[which]) for which, (src, dst) in enumerate(pairs)]
    for move in moves:
        move.start()
    count = coef.shape[0]
    per, width = zs.shape[1], zs.shape[-1]
    n = ITERS
    rows_in = [known[k] for k in range(3 * n)]
    bias_part, soft_part = mixing(rows_in[:n], rows_in[n : 2 * n - 1], rows_in[2 * n - 1 : 3 * n - 1], rows_in[3 * n - 1], unit_count, coef, 0)

    def final(s, carry):
        cf = [coef[k, pl.ds(s, 1), :] for k in range(count)]

        def parts(cols):
            return [[ref[i, s, :, cols] for i in range(ITERS)] for ref in (zs, ims)]

        def put(cols, values):
            for which, val in enumerate(values):
                new[which, s, :, cols] = val

        gradients(cf, width // LANES, parts, put)
        return carry

    lax.fori_loop(0, per, final, 0, unroll=2)
    moves += [pltpu.make_async_copy(new.at[which], dst.at[CHUNKS - 1], sems.at[3 + which]) for which, (_, dst) in enumerate(pairs)]
    for move in moves[3:]:
        move.start()
    fetch.wait()
    specs = gbias.shape[0]
    lane = lax.broadcasted_iota(jnp.int32, (per, LANES), 1)
    mine = lane == (CHUNKS - 1) * per + lax.broadcasted_iota(jnp.int32, (per, LANES), 0)
    for k, (row, part) in enumerate(((row_b, bias_part), (row_s, soft_part))):
        whole = sums[k : k + 1, :] + jnp.sum(jnp.where(mine, part, 0.0), axis=0, keepdims=True)
        row[...] = whole[0, :specs]
    rows = [pltpu.make_async_copy(row_b, gbias, sems.at[6]), pltpu.make_async_copy(row_s, soft, sems.at[7])]
    for row in rows:
        row.start()
    for move in moves + rows:
        move.wait()


def in_hbm(array):
    return pltpu.with_memory_space_constraint(array, pltpu.HBM)


def body(start_lead, start_field, diag_dual, coupling_dual, linear_table, labels, bias_dual, kernels):
    sections = lax.axis_size("layer")
    specs, _, rows, width = start_field.shape
    unit_count = sections * rows * width
    per = specs // CHUNKS
    chan = kernels.shape[-1]
    block = (per, rows, width)
    shape = (CHUNKS,) + block
    full = pl.BlockSpec(memory_space=pltpu.VMEM)
    anywhere = pl.BlockSpec(memory_space=pl.ANY)
    f32, bf16 = jnp.float32, jnp.bfloat16
    dma = pltpu.SemaphoreType.DMA
    slots, sent = ITERS * CHUNKS, (ITERS - 1) * CHUNKS
    small_block = (per, LANES)
    outs = pl.pallas_call(
        functools.partial(kernel_body, sections, float(unit_count)),
        out_shape=[pltpu.VMEM(shape, f32)] * 3 + [pltpu.VMEM((2, LANES), f32)] + [pltpu.VMEM((ITERS,) + block, f32)] * 2 + [pltpu.VMEM((3 * ITERS,) + small_block, f32)],
        in_specs=[anywhere] * 8,
        out_specs=[full] * 7,
        scratch_shapes=[
            pltpu.VMEM((slots,) + block, f32),
            pltpu.VMEM((slots,) + block, f32),
            pltpu.VMEM((sent,) + block, f32),
            pltpu.VMEM((slots,) + block, f32),
            pltpu.VMEM((sent,) + block, f32),
            pltpu.VMEM(shape, f32),
            pltpu.VMEM((sent,) + block, f32),
            pltpu.VMEM((per * rows, width + LANES), bf16),
            pltpu.VMEM((per * rows, width + LANES), bf16),
            pltpu.VMEM((4 * chan, 12 * chan), bf16),
            pltpu.VMEM((4 * chan, 12 * chan), bf16),
            pltpu.VMEM((4,) + small_block, f32),
            pltpu.VMEM((24,) + small_block, f32),
            pltpu.VMEM((slots,) + small_block, f32),
            pltpu.VMEM((slots,) + small_block, f32),
            pltpu.VMEM((slots,) + small_block, f32),
            pltpu.VMEM((CHUNKS,) + small_block, f32),
            pltpu.VMEM((2 * CHUNKS, 1, LANES), f32),
            pltpu.VMEM((2 * CHUNKS, sections, 1, LANES), f32),
            pltpu.VMEM((slots, per - per // 2, rows, width), f32),
            pltpu.VMEM(shape, f32),
            pltpu.VMEM(shape, f32),
            pltpu.VMEM((linear_table.shape[0], rows, width), f32),
            pltpu.VMEM(kernels.shape[1:], f32),
            dma((slots,)),
            dma((slots,)),
            dma((sent,)),
            dma((sent,)),
            dma((2 * CHUNKS, sections)),
            dma((2 * CHUNKS, sections)),
            dma((slots,)),
            dma((slots,)),
            dma((slots,)),
            dma((slots,)),
            pltpu.SMEM((specs,), jnp.int32),
            pltpu.SMEM((specs,), f32),
            pltpu.SMEM((specs,), f32),
            dma((3, CHUNKS)),
            dma((5,)),
            dma((2, ITERS)),
        ],
        compiler_params=pltpu.CompilerParams(collective_id=0, has_side_effects=True, vmem_limit_bytes=44 * 1024 * 1024),
    )(
        in_hbm(labels),
        in_hbm(start_lead),
        in_hbm(bias_dual),
        in_hbm(start_field.reshape(shape)),
        in_hbm(diag_dual.reshape(shape)),
        in_hbm(coupling_dual.reshape(shape)),
        in_hbm(linear_table.reshape(linear_table.shape[0], rows, width)),
        in_hbm(kernels.reshape(kernels.shape[1:])),
    )
    done = pl.pallas_call(
        functools.partial(hand_over, float(unit_count)),
        out_shape=[jax.ShapeDtypeStruct(shape, f32)] * 3 + [jax.ShapeDtypeStruct((specs,), f32)] * 2,
        in_specs=[anywhere] * 4 + [full] * 3,
        out_specs=[anywhere] * 5,
        scratch_shapes=[pltpu.VMEM((2, LANES), f32), pltpu.VMEM((specs,), f32), pltpu.VMEM((specs,), f32), pltpu.VMEM((3,) + block, f32), pltpu.VMEM((20,) + small_block, f32), dma((9,))],
        compiler_params=pltpu.CompilerParams(vmem_limit_bytes=8 * 1024 * 1024),
    )(*outs)
    big = [out.reshape(start_field.shape) for out in done[:3]]
    return (*big, done[3], done[4])


def solution(mesh):
    placed = (
        P("spec"),
        P("spec", "layer", None, None),
        P("spec", "layer", None, None),
        P("spec", "layer", None, None),
        P(None, "layer", None, None),
        P("spec"),
        P("spec"),
        P("layer", None, None, None, None),
    )
    return jax.shard_map(
        body,
        mesh=mesh,
        in_specs=placed,
        out_specs=(
            P("spec", "layer", None, None),
            P("spec", "layer", None, None),
            P("spec", "layer", None, None),
            P("spec"),
            P("spec"),
        ),
        check_vma=False,
    )
```
